256 devices in a mesh: tok: 16 (over y_lo, x, core), mdl: 16 (over y_hi, z).
Axes of the slice: x: 4, y: 4 (y_hi: 2, y_lo: 2; y = y_hi * 2 + y_lo), z: 8, core: 2. Of those that a mesh axis runs over, the one named last changes fastest.
Arguments:
- hidden: bfloat16 [8192, 2048], P('tok'), may hold values from -40 to 40
- segment_ids: int32 [8192], replicated, may hold values from 0 to 3, never falling along the last dimension, each value on 1 to 4096 neighbouring positions
- routes: int32 [8192, 2], P('tok'), may hold values from 0 to 7, all different within a row; in each aligned block of 512 rows (0 to 511, 512 to 1023, ...) at most 256 rows name the same one
- norm_gain: float32 [2048], replicated, may hold values from 0.5 to 1.5
- router_weight: float32 [2048, 8], replicated, may hold values from -0.125 to 0.125
- query_weight: bfloat16 [8, 2048, 2048], P(None, 'tok', 'mdl'), may hold values from -2 to 2
- kv_weight: bfloat16 [2, 2048, 2048], P(None, 'tok', 'mdl'), may hold values from -16 to 16
- out_weight: bfloat16 [8, 2048, 2048], P(None, 'mdl', 'tok'), may hold values from -0.5 to 0.5
- page_table: int32 [512], P('tok'), may hold values from 0 to 511, as said below
Outputs:
- output: bfloat16 [8192, 2048], P('tok', 'mdl')
- cache: bfloat16 [512, 16, 2, 2048], P('tok', None, None, 'mdl')
The draws below stay inside these ranges and needn't reach their ends.
Inputs may be any that keep to these rules, and one draw needn't show every extreme that they name: `segment_ids`: Non-decreasing along the tokens; every prompt number 0 to 3 occurs, each prompt 1 to 4096 tokens long, one exactly 4096. `routes`: each token names 2 different experts; among the 512 tokens of an aligned block no expert is named more than 256 times, and some block reaches 256. `page_table`: A permutation of the 512 physical pages; of the 32 logical pages of each aligned block, exactly 2 lie in each aligned range of 32 physical pages.
All inputs are finite; a program needn't handle non-finite values.
Results may differ from the reference program's by a relative error of at most 0.019.
Values may be sent and summed in bfloat16 or wider, within the bound.
No kernel may reach another device: no remote copies, remote signals or barrier semaphores. Data moves between devices by JAX's collectives and lax.ppermute only.
A program may use at most 128 MiB of HBM per device.

```python
import math
import jax
import jax.numpy as jnp
import numpy as np
from jax import lax

D = 2048
HEADS = 16
HDIM = 128
AEXP = 8
ATOP = 2
PAGE = 16
SEGS = 4
TOK_DEV = 512
TOKENS = 8192
MOST_LEN = 4096
CAP = 256
PG_DEV = 32
PAGES = 512
SHARDS = 16
N_MDL = 16


def loguniform_draw(key, shape, lowest, highest):
    return jnp.exp(jax.random.uniform(key, shape, jnp.float32, math.log(lowest), math.log(highest)))


def clipped_normal(key, shape, bound_value):
    return jnp.clip(jax.random.normal(key, shape, jnp.float32), -bound_value, bound_value)


def draw_hidden(key, part):
    columns = loguniform_draw(jax.random.fold_in(key, 1), (D,), 0.3, 3.0)
    base = clipped_normal(jax.random.fold_in(key, 2), (TOKENS, D), 6.0)
    values = base * columns[None, :]
    return values.astype(jnp.bfloat16)


def attention_weights(key):
    factor = 2.0 / math.sqrt(D)
    queries = clipped_normal(jax.random.fold_in(key, 21), (AEXP, D, HEADS * HDIM), 5.0) * factor
    keys = clipped_normal(jax.random.fold_in(key, 22), (D, HEADS * HDIM), 5.0) * factor
    values = clipped_normal(jax.random.fold_in(key, 23), (D, HEADS * HDIM), 5.0) / math.sqrt(D)
    return (queries, jnp.stack([keys, values]))


def draw_query_weight(key, part):
    return attention_weights(key)[0].astype(jnp.bfloat16)


def draw_kv_weight(key, part):
    return attention_weights(key)[1].astype(jnp.bfloat16)


def one_permutation(subkey):
    return jax.random.permutation(subkey, PG_DEV)


def draw_page_table(key, part):
    per_peer = PG_DEV // SHARDS
    source_ranks = jax.vmap(one_permutation)(jax.random.split(jax.random.fold_in(key, 31), SHARDS))
    target_orders = jax.vmap(one_permutation)(jax.random.split(jax.random.fold_in(key, 32), SHARDS))
    targets = source_ranks // per_peer
    within = source_ranks % per_peer
    sources = jnp.arange(SHARDS, dtype=jnp.int32)[:, None]
    local_page = target_orders[targets, sources * per_peer + within]
    return (targets * PG_DEV + local_page).reshape(PAGES).astype(jnp.int32)


def steps_of(stream_key, extent, cuts, smallest, top_value):
    gain, own = 1.0, jax.random.fold_in(stream_key, 6)
    for axis_at, shards_of in cuts:
        heights = jnp.exp(jax.random.uniform(jax.random.fold_in(own, axis_at), (shards_of,), jnp.float32, smallest / len(cuts), top_value / len(cuts)))
        gain = gain * jnp.repeat(heights, extent[axis_at] // shards_of).reshape([-1 if axis == axis_at else 1 for axis in range(len(extent))])
    return gain


def length_profile(amount, total, limit, lean):
    portions = [(1 << 20) // math.isqrt(rank ** lean) + 1 for rank in range(2, amount + 1)]
    surplus, given = total - limit - (amount - 1), [1] * (amount - 1)
    while surplus > 0:
        free = [i for i in range(amount - 1) if given[i] < limit]
        mass, budget = sum([portions[i] for i in free]), surplus
        for i in free:
            addition = min(limit - given[i], max(1, budget * portions[i] // mass), surplus)
            given[i] = given[i] + addition
            surplus = surplus - addition
    return np.array([limit] + given)


def ragged_sizes(stream_key, amount, total, most, lean):
    if amount == 2:
        one = jax.random.randint(stream_key, (), max(1, total - most), min(most, total - 1) + 1)
        return jnp.stack([one, total - one])
    sizes = jnp.asarray(length_profile(amount, total, most, lean), jnp.int32)
    pairs = (amount - 1) // 2
    giver, receiver = sizes[1:1 + 2 * pairs:2], sizes[2:2 + 2 * pairs:2]
    room = jnp.minimum(giver - 1, most - receiver)
    passed = jax.random.randint(jax.random.fold_in(stream_key, 1), (pairs,), 0, 1 << 20) % (room + 1)
    sizes = sizes.at[1:1 + 2 * pairs:2].set(giver - passed).at[2:2 + 2 * pairs:2].set(receiver + passed)
    return sizes[jax.random.permutation(jax.random.fold_in(stream_key, 2), amount)]


def deal_out(stream_key, own, number, rows, number_of, top, bound, slope):
    order = jax.random.permutation(stream_key, number_of)
    heavy_load, common = shares(number_of, rows * top, bound, slope, True), shares(number_of, rows * top, bound, slope, False)
    places = jnp.arange(number_of)

    def named(sizes, turn):
        used = int((sizes > 0).sum())
        fixed = max(1, used // 4)
        shifted = fixed + (places - fixed + turn * (used - fixed)) % max(1, number_of - fixed)
        return jnp.zeros((number_of,), jnp.int32).at[order[jnp.where(places < fixed, places, shifted)]].set(jnp.asarray(sizes, jnp.int32))

    sizes = jnp.where(number % 4 == 0, named(heavy_load, number // 4), named(common, number - number // 4 - 1))
    mixed = jax.random.permutation(jax.random.fold_in(own, 3), number_of)
    giver, receiver = mixed[0:number_of // 2 * 2:2], mixed[1:number_of // 2 * 2:2]
    margin = jnp.minimum(sizes[giver] - 1, bound - sizes[receiver]) // 2
    margin = jnp.where((giver == order[0]) | (receiver == order[0]) | (sizes[receiver] == 0), 0, jnp.maximum(margin, 0))
    shifted = jax.random.randint(jax.random.fold_in(own, 4), (number_of // 2,), 0, 1 << 20) % (margin + 1)
    sizes = sizes.at[giver].add(-shifted).at[receiver].add(shifted)
    members = jnp.searchsorted(jnp.cumsum(sizes), jnp.arange(rows * top), side="right").astype(jnp.int32)
    listing = members.reshape(top, rows).T
    listing = listing[jax.random.permutation(jax.random.fold_in(own, 1), rows)]
    turn = jax.random.randint(jax.random.fold_in(own, 2), (rows, 1), 0, top)
    return jnp.take_along_axis(listing, (jnp.arange(top)[None, :] + turn) % top, axis=1)


def shares(number_of, total, bound, skew, full):
    portions = [(1 << 20) // math.isqrt(standing ** skew) + 1 for standing in range(1, number_of + 1)]
    largest = bound if full else min(bound, max(-(-total // number_of), total * portions[0] // sum(portions)))
    least = 1 if total - largest >= number_of - 1 else 0
    holding, surplus = [largest] + [least] * (number_of - 1), total - largest - least * (number_of - 1)
    while surplus > 0:
        candidates = [i for i in range(1, number_of) if holding[i] < largest] or [i for i in range(1, number_of) if holding[i] < bound]
        mass, budget = sum([portions[i] for i in candidates]), surplus
        for i in candidates:
            more = min(bound - holding[i], max(1, budget * portions[i] // mass), surplus)
            holding[i] = holding[i] + more
            surplus = surplus - more
    return np.array(holding)


def noise(key, extent, width, bound, cuts=(), kind=jnp.bfloat16):
    drawn = width * jax.random.normal(key, extent, jnp.float32)
    if cuts:
        drawn = drawn * steps_of(key, extent, cuts, -0.22, 0.18)
    return jnp.clip(drawn, -bound, bound).astype(kind)


def setup_inputs(seed: int = 0) -> dict:
    seeds = jax.random.split(jax.random.key(seed), 10)
    hidden = draw_hidden(jax.random.fold_in(seeds[9], 71), 0)
    segment_ids = jnp.searchsorted(jnp.cumsum(ragged_sizes(seeds[1], SEGS, TOKENS, MOST_LEN, 2)), jnp.arange(TOKENS), side="right").astype(jnp.int32)
    routes_keys = jax.random.split(jax.random.fold_in(seeds[2], 1), TOKENS // TOK_DEV)
    routes_turns = jax.random.permutation(jax.random.fold_in(seeds[2], 3), TOKENS // TOK_DEV)
    routes = jax.vmap(lambda own, number: deal_out(jax.random.fold_in(seeds[2], 2), own, number, TOK_DEV, AEXP, ATOP, CAP, 1))(routes_keys, routes_turns).reshape((TOKENS, ATOP))
    norm_gain = jnp.clip(1.0 + 0.1 * jax.random.normal(seeds[3], (D,), jnp.float32), 0.5, 1.5)
    router_weight = noise(seeds[4], (D, AEXP), D ** -0.5, 0.125, (), jnp.float32)
    query_weight = draw_query_weight(jax.random.fold_in(seeds[9], 71), 0)
    kv_weight = draw_kv_weight(jax.random.fold_in(seeds[9], 71), 0)
    out_weight = noise(seeds[7], (AEXP, HEADS * HDIM, D), (HEADS * HDIM // 16) ** -0.5, 0.5, ((1, 16), (2, 16)))
    page_table = draw_page_table(jax.random.fold_in(seeds[9], 71), 0)
    return dict(hidden=hidden, segment_ids=segment_ids, routes=routes, norm_gain=norm_gain, router_weight=router_weight, query_weight=query_weight, kv_weight=kv_weight, out_weight=out_weight, page_table=page_table)


EPSILON = 1e-05
MASKED = -1e+30

def rms_norm(hidden, norm_gain):
    values = hidden.astype(jnp.float32)
    factor = lax.rsqrt(lax.optimization_barrier(jnp.mean(values * values, axis=-1, keepdims=True)) + EPSILON)
    return (values * factor * norm_gain).astype(jnp.bfloat16)

def route_gates(normed, router_weight, routes):
    logits = jnp.dot(normed.astype(jnp.float32), router_weight, precision=lax.Precision.HIGHEST)
    expert_ids = jnp.arange(logits.shape[1], dtype=jnp.int32)
    picked = routes[:, :, None] == expert_ids[None, None, :]
    chosen = lax.optimization_barrier(jnp.sum(jnp.where(picked, logits[:, None, :], jnp.float32(0.0)), axis=-1))
    return jax.nn.softmax(chosen, axis=-1)

def reference(hidden, segment_ids, routes, norm_gain, router_weight, query_weight, kv_weight, out_weight, page_table):
    head_cols = HEADS * HDIM
    normed = rms_norm(hidden, norm_gain)
    gates = route_gates(normed, router_weight, routes)
    key_values = jnp.stack([jnp.dot(normed, kv_weight[0], preferred_element_type=jnp.float32), jnp.dot(normed, kv_weight[1], preferred_element_type=jnp.float32)], axis=1).astype(jnp.bfloat16)

    def expert_queries(carry, expert):
        projected = jnp.dot(normed, query_weight[expert], preferred_element_type=jnp.float32).astype(jnp.bfloat16)
        return (jnp.where((routes == expert)[:, :, None], projected[:, None, :], carry), None)
    queries, _ = lax.scan(expert_queries, jnp.zeros((TOKENS, ATOP, head_cols), jnp.bfloat16), jnp.arange(AEXP, dtype=jnp.int32))
    query_block = math.gcd(TOKENS, 1024)
    window = min(TOKENS, MOST_LEN + query_block)
    blocks = TOKENS // query_block
    by_head_q = queries.reshape(TOKENS, ATOP, HEADS, HDIM).transpose(2, 1, 0, 3)
    by_head_k = key_values[:, 0].reshape(TOKENS, HEADS, HDIM).transpose(1, 0, 2)
    by_head_v = key_values[:, 1].reshape(TOKENS, HEADS, HDIM).transpose(1, 0, 2)
    zero_index = jnp.zeros((), jnp.int32)

    def attend(index):
        head = (index // blocks).astype(jnp.int32)
        first = (index % blocks * query_block).astype(jnp.int32)
        key_first = jnp.clip(first + query_block - window, 0, TOKENS - window).astype(jnp.int32)
        q_rows = lax.dynamic_slice(by_head_q, (head, zero_index, first, zero_index), (1, ATOP, query_block, HDIM))[0].astype(jnp.float32)
        k_rows = lax.dynamic_slice(by_head_k, (head, key_first, zero_index), (1, window, HDIM))[0].astype(jnp.float32)
        v_rows = lax.dynamic_slice(by_head_v, (head, key_first, zero_index), (1, window, HDIM))[0].astype(jnp.float32)
        q_seg = lax.dynamic_slice(segment_ids, (first,), (query_block,))
        k_seg = lax.dynamic_slice(segment_ids, (key_first,), (window,))
        q_pos = first + jnp.arange(query_block, dtype=jnp.int32)
        k_pos = key_first + jnp.arange(window, dtype=jnp.int32)
        allowed = (q_seg[:, None] == k_seg[None, :]) & (k_pos[None, :] <= q_pos[:, None])
        scores = jnp.einsum('sqd,kd->sqk', q_rows, k_rows) / math.sqrt(HDIM)
        scores = jnp.where(allowed[None], scores, jnp.float32(MASKED))
        peak = lax.optimization_barrier(jnp.max(scores, axis=-1, keepdims=True))
        expon = jnp.where(allowed[None], jnp.exp(scores - peak), jnp.float32(0.0))
        totals = lax.optimization_barrier(jnp.sum(expon, axis=-1, keepdims=True))
        probs = expon.astype(jnp.bfloat16).astype(jnp.float32)
        return (jnp.einsum('sqk,kd->sqd', probs, v_rows) / totals).astype(jnp.bfloat16)
    attended = lax.map(attend, jnp.arange(HEADS * blocks, dtype=jnp.int32))
    attended = attended.reshape(HEADS, blocks, ATOP, query_block, HDIM).transpose(1, 3, 2, 0, 4).reshape(TOKENS, ATOP, head_cols)
    group_cols = head_cols // N_MDL

    def group_output(total, group):
        col_first = (group * group_cols).astype(jnp.int32)
        group_rows = lax.dynamic_slice_in_dim(attended, col_first, group_cols, 2)

        def expert_output(partial_value, expert):
            chosen = routes == expert
            rows = lax.optimization_barrier(jnp.sum(jnp.where(chosen[:, :, None], group_rows.astype(jnp.float32), jnp.float32(0.0)), axis=1)).astype(jnp.bfloat16)
            weight = lax.optimization_barrier(jnp.sum(jnp.where(chosen, gates, jnp.float32(0.0)), axis=1))
            block = lax.dynamic_slice_in_dim(out_weight[expert], col_first, group_cols, 0)
            return (partial_value + weight[:, None] * jnp.dot(rows, block, preferred_element_type=jnp.float32), None)
        partial_value, _ = lax.scan(expert_output, jnp.zeros((TOKENS, D), jnp.float32), jnp.arange(AEXP, dtype=jnp.int32))
        rounded = lax.optimization_barrier(partial_value.astype(jnp.bfloat16))
        return (total + rounded.astype(jnp.float32), None)
    mixed, _ = lax.scan(group_output, jnp.zeros((TOKENS, D), jnp.float32), jnp.arange(N_MDL, dtype=jnp.int32))
    output = (hidden.astype(jnp.float32) + mixed).astype(jnp.bfloat16)
    logical = key_values.reshape(PAGES, PAGE, 2, head_cols)
    cache = jnp.zeros_like(logical).at[page_table].set(logical)
    return (output, cache)
```

```python
import math

import jax
import jax.numpy as jnp
from jax import lax
from jax.experimental import pallas as pl
from jax.experimental.pallas import tpu as pltpu
from jax.sharding import PartitionSpec as P

HDIM = 128
SEGS = 4
EPSILON = 1e-05
MASKED = -1e30
KEY_BLOCK = 512
QUERY_BLOCK = 256
WINDOW_PAIRS = 5
QUERY_SCALE = math.log2(math.e) / math.sqrt(HDIM)


def rms_norm(hidden, norm_gain):
    values = hidden.astype(jnp.float32)
    factor = lax.rsqrt(jnp.mean(values * values, axis=-1, keepdims=True) + EPSILON)
    return (values * factor * norm_gain).astype(jnp.bfloat16)


def route_weights(normed, router_weight, routes):
    logits = jnp.dot(normed.astype(jnp.float32), router_weight, precision=lax.Precision.HIGHEST)
    expert_ids = jnp.arange(logits.shape[1], dtype=jnp.int32)
    picked = routes[:, :, None] == expert_ids[None, None, :]
    chosen = jnp.sum(jnp.where(picked, logits[:, None, :], jnp.float32(0.0)), axis=-1)
    gates = jax.nn.softmax(chosen, axis=-1)
    return jnp.where(picked, gates[:, :, None], 0.0).reshape(routes.shape[0], -1)


def place_pages(key_values, page_table, shards, tok_row):
    pages_here = page_table.shape[0]
    per_peer = pages_here // shards
    rows = key_values.shape[0] // pages_here
    cols = key_values.shape[1]
    targets = page_table // pages_here
    onehot = (targets[:, None] == jnp.arange(shards, dtype=jnp.int32)[None, :]).astype(jnp.int32)
    ranks = jnp.sum((jnp.cumsum(onehot, axis=0) - 1) * onehot, axis=1)
    ordering = (
        jnp.zeros((pages_here,), jnp.int32)
        .at[targets * per_peer + ranks]
        .set(jnp.arange(pages_here, dtype=jnp.int32))
    )
    outgoing = key_values.reshape(pages_here, rows, cols)[ordering].reshape(
        shards, per_peer, rows, cols
    )
    labels = page_table[ordering].reshape(shards, per_peer)
    incoming = lax.all_to_all(outgoing, "tok", split_axis=0, concat_axis=0, tiled=True)
    got_labels = lax.all_to_all(labels, "tok", split_axis=0, concat_axis=0, tiled=True)
    places = got_labels.reshape(-1) - tok_row * pages_here
    order = jnp.zeros((pages_here,), jnp.int32).at[places].set(
        jnp.arange(pages_here, dtype=jnp.int32)
    )
    return incoming.reshape(pages_here, rows, 2, cols // 2)[order]


def query_body(normed_ref, weight_ref, routes_ref, out_ref):
    step = pl.program_id(0)
    chunks, pair, rows, cols = weight_ref.shape
    weights = [weight_ref[:, k].reshape(chunks * rows, cols) for k in range(pair)]
    total = jnp.dot(
        normed_ref[...], jnp.concatenate(weights, axis=1), preferred_element_type=jnp.float32
    )
    for s in range(out_ref.shape[0]):
        route = routes_ref[:, s : s + 1]
        value = out_ref[s]
        for k in range(pair):
            mine = (total[:, k * cols : (k + 1) * cols] * QUERY_SCALE).astype(jnp.bfloat16)
            value = jnp.where(route == step * pair + k, mine, value)
        out_ref[s] = value


def project_queries(normed, gathered, routes, experts):
    tokens, width = normed.shape
    shards, _, rows, cols = gathered.shape
    return pl.pallas_call(
        query_body,
        grid=(experts // 2,),
        in_specs=[
            pl.BlockSpec((tokens, width), lambda e: (0, 0)),
            pl.BlockSpec((shards, 2, rows, cols), lambda e: (0, e, 0, 0)),
            pl.BlockSpec(routes.shape, lambda e: (0, 0)),
        ],
        out_specs=pl.BlockSpec((routes.shape[1], tokens, cols), lambda e: (0, 0, 0)),
        out_shape=jax.ShapeDtypeStruct((routes.shape[1], tokens, cols), jnp.bfloat16),
    )(normed, gathered, routes)


def attend_body(bounds_ref, q_ref, lower_ref, place_ref, kv_ref, out_ref):
    step = pl.program_id(0)
    routes, tokens, dim = q_ref.shape
    rows = routes * tokens
    q = q_ref[...].reshape(rows, dim)
    lower = jnp.concatenate([lower_ref[...]] * routes, axis=0)
    place = jnp.concatenate([place_ref[...]] * routes, axis=0)

    def block(masked, at, carry):
        peak, total, accum = carry
        first = pl.multiple_of(at * KEY_BLOCK, KEY_BLOCK)
        keys = kv_ref[pl.ds(first, KEY_BLOCK), :dim]
        values = kv_ref[pl.ds(first, KEY_BLOCK), dim:]
        scores = lax.dot_general(
            q, keys, (((1,), (1,)), ((), ())), preferred_element_type=jnp.float32
        )
        if masked:
            key_place = first + lax.broadcasted_iota(jnp.int32, (1, KEY_BLOCK), 1)
            allowed = (key_place >= lower) & (key_place <= place)
            scores = jnp.where(allowed, scores, MASKED)
        new_peak = jnp.maximum(peak, jnp.max(scores, axis=1, keepdims=True))
        shrink = jnp.exp2(peak - new_peak)
        expon = jnp.exp2(scores - new_peak)
        total = total * shrink + jnp.sum(expon, axis=1, keepdims=True)
        accum = accum * shrink + jnp.dot(
            expon.astype(jnp.bfloat16), values, preferred_element_type=jnp.float32
        )
        return new_peak, total, accum

    state = (
        jnp.full((rows, 1), MASKED, jnp.float32),
        jnp.zeros((rows, 1), jnp.float32),
        jnp.zeros((rows, dim), jnp.float32),
    )
    start, full, edge, stop = (bounds_ref[4 * step + k] for k in range(4))
    state = lax.fori_loop(start, full, lambda at, c: block(True, at, c), state)
    state = lax.fori_loop(full, edge, lambda at, c: block(False, at, c), state)
    state = lax.fori_loop(edge, stop, lambda at, c: block(True, at, c), state)
    out_ref[...] = (state[2] / state[1]).astype(jnp.bfloat16).reshape(routes, tokens, dim)


def attend(queries, lower, place, window):
    routes, tokens, dim = queries.shape
    steps = tokens // QUERY_BLOCK
    first_lower = lower.reshape(steps, QUERY_BLOCK)[:, 0]
    last_lower = lower.reshape(steps, QUERY_BLOCK)[:, -1]
    first_place = place.reshape(steps, QUERY_BLOCK)[:, 0]
    last_place = place.reshape(steps, QUERY_BLOCK)[:, -1]
    start = first_lower // KEY_BLOCK
    stop = last_place // KEY_BLOCK + 1
    full = jnp.clip((last_lower + KEY_BLOCK - 1) // KEY_BLOCK, start, stop)
    edge = jnp.clip((first_place + 1) // KEY_BLOCK, full, stop)
    bounds = jnp.stack([start, full, edge, stop], axis=1).reshape(-1)
    return pl.pallas_call(
        attend_body,
        grid_spec=pltpu.PrefetchScalarGridSpec(
            num_scalar_prefetch=1,
            grid=(steps,),
            in_specs=[
                pl.BlockSpec((routes, QUERY_BLOCK, dim), lambda i, b: (0, i, 0)),
                pl.BlockSpec((QUERY_BLOCK, 1), lambda i, b: (i, 0)),
                pl.BlockSpec((QUERY_BLOCK, 1), lambda i, b: (i, 0)),
                pl.BlockSpec(window.shape, lambda i, b: (0, 0)),
            ],
            out_specs=pl.BlockSpec((routes, QUERY_BLOCK, dim), lambda i, b: (0, i, 0)),
        ),
        out_shape=jax.ShapeDtypeStruct((routes, tokens, dim), jnp.bfloat16),
    )(bounds, queries, lower[:, None], place[:, None], window)


def mix_body(side_ref, own_ref, peer_ref, gates_ref, own_weight_ref, peer_weight_ref, out_ref, mix_ref):
    del side_ref
    experts, rows, cols = own_weight_ref.shape[2:]
    routes = own_ref.shape[0]

    @pl.when(pl.program_id(0) == 0)
    def _():
        for h, ref in enumerate((own_ref, peer_ref)):
            attended = [ref[s].astype(jnp.float32) for s in range(routes)]
            for e in range(experts):
                value = sum(
                    attended[s] * gates_ref[:, s * experts + e : s * experts + e + 1]
                    for s in range(routes)
                )
                mix_ref[h, :, e * rows : (e + 1) * rows] = value.astype(jnp.bfloat16)

    total = jnp.zeros((out_ref.shape[1], 2 * cols), jnp.float32)
    for h, ref in enumerate((own_weight_ref, peer_weight_ref)):
        weight = jnp.concatenate(
            [ref[0, k].reshape(experts * rows, cols) for k in range(2)], axis=1
        )
        total = total + jnp.dot(mix_ref[h], weight, preferred_element_type=jnp.float32)
    for k in range(2):
        out_ref[k] = total[:, k * cols : (k + 1) * cols].astype(jnp.bfloat16)


def mix_heads(side, own, peer, gates, gathered, experts):
    routes, tokens, dim = own.shape
    _, chunks, _, rows, cols = gathered.shape
    block = (1, 2, experts, rows, cols)
    whole = lambda i, s: (0, 0, 0)
    return pl.pallas_call(
        mix_body,
        grid_spec=pltpu.PrefetchScalarGridSpec(
            num_scalar_prefetch=1,
            grid=(chunks // 2,),
            in_specs=[
                pl.BlockSpec((routes, tokens, dim), whole),
                pl.BlockSpec((routes, tokens, dim), whole),
                pl.BlockSpec(gates.shape, lambda i, s: (0, 0)),
                pl.BlockSpec(block, lambda i, s: (s[0], i, 1, 0, 0)),
                pl.BlockSpec(block, lambda i, s: (1 - s[0], i, 1, 0, 0)),
            ],
            out_specs=pl.BlockSpec((2, tokens, cols), lambda i, s: (i, 0, 0)),
            scratch_shapes=[pltpu.VMEM((2, tokens, experts * rows), jnp.bfloat16)],
        ),
        out_shape=jax.ShapeDtypeStruct((chunks, tokens, cols), jnp.bfloat16),
    )(side, own, peer, gates, gathered, gathered)


def local(
    hidden,
    segment_ids,
    routes,
    norm_gain,
    router_weight,
    query_weight,
    kv_weight,
    out_weight,
    page_table,
):
    tok_dev, width = hidden.shape
    experts, chunk, head_cols = query_weight.shape
    shards = lax.axis_size("tok")
    groups = lax.axis_size("mdl")
    half_tok, half_mdl = shards // 2, groups // 2
    tok_row = lax.axis_index("tok")
    mdl_row = lax.axis_index("mdl")
    core = tok_row % 2
    pair = tok_row // 2
    side = mdl_row // half_mdl

    swap = [
        ((a * half_tok + i) * groups + b * half_mdl + z, (b * half_tok + i) * groups + a * half_mdl + z)
        for a in range(2)
        for b in range(2)
        for i in range(half_tok)
        for z in range(half_mdl)
    ]
    out_block = lax.ppermute(out_weight, ("tok", "mdl"), swap)
    blocks = jnp.concatenate([query_weight, out_block], axis=0)
    gathered = lax.all_gather(blocks, "tok", axis=0)

    same_core = [[2 * k + c for k in range(half_tok)] for c in range(2)]
    core_swap = [(i, i ^ 1) for i in range(shards)]
    kv_mine = lax.all_to_all(
        jnp.broadcast_to(kv_weight[None], (half_tok,) + kv_weight.shape),
        "tok", 0, 0, axis_index_groups=same_core, tiled=True,
    )
    kv_other = lax.ppermute(kv_mine, "tok", core_swap)
    first = core == 0
    kv_blocks = jnp.stack(
        [jnp.where(first, kv_mine, kv_other), jnp.where(first, kv_other, kv_mine)], axis=1
    )
    kv_full = kv_blocks.transpose(0, 1, 3, 2, 4).reshape(width, 2 * head_cols)
    normed = rms_norm(hidden, norm_gain)
    key_values = jnp.dot(normed, kv_full, preferred_element_type=jnp.float32).astype(jnp.bfloat16)

    earlier = [
        lax.ppermute(key_values, "tok", [(i, i + 2 * s) for i in range(shards - 2 * s)])
        for s in range(WINDOW_PAIRS - 1, 0, -1)
    ]
    mine = jnp.stack(earlier + [key_values])
    other = lax.ppermute(mine, "tok", core_swap)
    window = jnp.stack(
        [jnp.where(first, mine, other), jnp.where(first, other, mine)], axis=1
    ).reshape(2 * WINDOW_PAIRS * tok_dev, 2 * head_cols)
    cache = place_pages(key_values, page_table, shards, tok_row)

    window_first = (pair - (WINDOW_PAIRS - 1)) * 2 * tok_dev
    own_first = tok_row * tok_dev
    own_segments = lax.dynamic_slice_in_dim(segment_ids, own_first, tok_dev)
    prompt_ids = jnp.arange(SEGS, dtype=jnp.int32)
    seg_first = jnp.sum((segment_ids[:, None] < prompt_ids[None, :]).astype(jnp.int32), axis=0)
    lower = jnp.sum(
        jnp.where(own_segments[:, None] == prompt_ids[None, :], seg_first[None, :], 0), axis=1
    )
    place = own_first + jnp.arange(tok_dev, dtype=jnp.int32)
    gates = route_weights(normed, router_weight, routes)

    queries = project_queries(normed, gathered, routes, experts)
    attended = attend(queries, lower - window_first, place - window_first, window)
    peer = lax.ppermute(attended, "mdl", [(j, j ^ half_mdl) for j in range(groups)])
    partial_sums = mix_heads(
        side[None],
        attended,
        peer,
        gates,
        gathered.reshape(2, half_tok, 2 * experts, chunk, head_cols),
        experts,
    )
    sides = [[b * half_mdl + z for z in range(half_mdl)] for b in range(2)]
    arrived = lax.all_to_all(partial_sums, "mdl", 0, 0, axis_index_groups=sides, tiled=True)
    mixed = jnp.sum(arrived.astype(jnp.float32), axis=0)
    span = width // groups
    residual = lax.dynamic_slice_in_dim(hidden, mdl_row * span, span, 1)
    output = (residual.astype(jnp.float32) + mixed).astype(jnp.bfloat16)
    return (output, cache)


def solution(mesh):
    placed = (
        P("tok", None),
        P(),
        P("tok", None),
        P(),
        P(),
        P(None, "tok", "mdl"),
        P(None, "tok", "mdl"),
        P(None, "mdl", "tok"),
        P("tok"),
    )
    return jax.shard_map(
        local,
        mesh=mesh,
        in_specs=placed,
        out_specs=(P("tok", "mdl"), P("tok", None, None, "mdl")),
        check_vma=False,
    )
```

```python
import math

import jax
import jax.numpy as jnp
from jax import lax
from jax.experimental import pallas as pl
from jax.experimental.pallas import tpu as pltpu
from jax.sharding import PartitionSpec as P

HDIM = 128
CHUNK = 128
LABEL_ROWS = 16
CHIPS_X = 4
WINDOW_PAIRS = 5
SEGS = 4
EPSILON = 1e-05
MASKED = -1e30
KEY_BLOCK = 512
QUERY_BLOCK = 256
QUERY_SCALE = math.log2(math.e) / math.sqrt(HDIM)


def rms_norm(hidden, norm_gain):
    values = hidden.astype(jnp.float32)
    factor = lax.rsqrt(jnp.mean(values * values, axis=-1, keepdims=True) + EPSILON)
    return (values * factor * norm_gain).astype(jnp.bfloat16)


def route_weights(normed, router_weight, routes):
    logits = jnp.dot(normed.astype(jnp.float32), router_weight, precision=lax.Precision.HIGHEST)
    expert_ids = jnp.arange(logits.shape[1], dtype=jnp.int32)
    picked = routes[:, :, None] == expert_ids[None, None, :]
    chosen = jnp.sum(jnp.where(picked, logits[:, None, :], jnp.float32(0.0)), axis=-1)
    gates = jax.nn.softmax(chosen, axis=-1)
    return jnp.where(picked, gates[:, :, None], 0.0).reshape(routes.shape[0], -1)


def cost(flops, transcendentals, moved):
    return pl.CostEstimate(flops=flops, transcendentals=transcendentals, bytes_accessed=moved)


def kv_body(core_ref, normed_ref, mine_ref, other_ref, out_ref, weight_ref):
    @pl.when(pl.program_id(0) == 0)
    def _():
        first = core_ref[0] == 0
        for k in range(mine_ref.shape[0]):
            for m in range(2):
                at = slice(m * CHUNK, (m + 1) * CHUNK)
                mine, other = mine_ref[k, at], other_ref[k, at]
                row = 2 * k * CHUNK
                weight_ref[row : row + CHUNK, at] = jnp.where(first, mine, other)
                weight_ref[row + CHUNK : row + 2 * CHUNK, at] = jnp.where(first, other, mine)

    total = jnp.dot(normed_ref[...], weight_ref[...], preferred_element_type=jnp.float32)
    out_ref[...] = total.astype(jnp.bfloat16)


def project_kv(core, normed, mine, other):
    tokens, width = normed.shape
    chips, _, cols = mine.shape
    rows = tokens // 2
    whole = pl.BlockSpec((chips, 2 * CHUNK, cols), lambda i, c: (0, 0, 0))
    return pl.pallas_call(
        kv_body,
        grid_spec=pltpu.PrefetchScalarGridSpec(
            num_scalar_prefetch=1,
            grid=(2,),
            in_specs=[pl.BlockSpec((rows, width), lambda i, c: (i, 0)), whole, whole],
            out_specs=pl.BlockSpec((rows, 2 * cols), lambda i, c: (i, 0)),
            scratch_shapes=[pltpu.VMEM((width, 2 * cols), jnp.bfloat16)],
        ),
        out_shape=jax.ShapeDtypeStruct((tokens, 2 * cols), jnp.bfloat16),
        cost_estimate=cost(2 * tokens * width * 2 * cols, 0, 2 * tokens * width),
    )(core[None], normed, mine, other)


def owners_of(tok_row, half_tok):
    core, chip, row = tok_row % 2, tok_row // 2 % CHIPS_X, tok_row // half_tok
    owners = []
    for c in range(2):
        source = core ^ c
        for step in (0, 2 * source - 1, 1 - 2 * source, 2):
            at = (chip + CHIPS_X + step) % CHIPS_X * 2 + source
            owners += [(row ^ r) * half_tok + at for r in range(2)]
    return owners


def piece_refs(refs):
    return [ref.at[row] for ref in refs for row in range(2)]


def query_body(owner_ref, normed_ref, routes_ref, *refs):
    pieces, out_ref, ordered_ref = piece_refs(refs[:-2]), refs[-2], refs[-1]
    step = pl.program_id(0)
    pair = pieces[0].shape[0]
    cols = out_ref.shape[2]

    @pl.when(step == 0)
    def _():
        for k in range(len(pieces)):
            at = pl.ds(pl.multiple_of(owner_ref[k] * CHUNK, CHUNK), CHUNK)
            ordered_ref[:, k * CHUNK : (k + 1) * CHUNK] = normed_ref[:, at]

    weights = [jnp.concatenate([ref[k] for ref in pieces], axis=0) for k in range(pair)]
    total = jnp.dot(
        ordered_ref[...], jnp.concatenate(weights, axis=1), preferred_element_type=jnp.float32
    )
    for s in range(out_ref.shape[0]):
        route = routes_ref[:, s : s + 1]
        value = out_ref[s]
        for k in range(pair):
            mine = (total[:, k * cols : (k + 1) * cols] * QUERY_SCALE).astype(jnp.bfloat16)
            value = jnp.where(route == step * pair + k, mine, value)
        out_ref[s] = value


def project_queries(owners, normed, blocks, routes):
    tokens, width = normed.shape
    experts, rows, cols = blocks[0].shape[1:]
    return pl.pallas_call(
        query_body,
        grid_spec=pltpu.PrefetchScalarGridSpec(
            num_scalar_prefetch=1,
            grid=(experts // 2,),
            in_specs=[
                pl.BlockSpec((tokens, width), lambda e, r: (0, 0)),
                pl.BlockSpec(routes.shape, lambda e, r: (0, 0)),
            ]
            + [
                pl.BlockSpec((2, 2, rows, cols), lambda e, r: (0, e, 0, 0))
                for _ in blocks
            ],
            out_specs=pl.BlockSpec((routes.shape[1], tokens, cols), lambda e, r: (0, 0, 0)),
            scratch_shapes=[pltpu.VMEM((tokens, width), jnp.bfloat16)],
        ),
        out_shape=jax.ShapeDtypeStruct((routes.shape[1], tokens, cols), jnp.bfloat16),
        cost_estimate=cost(2 * tokens * width * experts * cols, 0, 4 * normed.size),
    )(owners, normed, routes, *blocks)


def attend_body(bounds_ref, q_ref, lower_ref, place_ref, *refs):
    block_refs, out_ref, kv_ref = refs[:-2], refs[-2], refs[-1]
    step = pl.program_id(0)
    routes, tokens, dim = q_ref.shape
    rows = routes * tokens
    half = len(block_refs) // 2
    core = bounds_ref[bounds_ref.shape[0] - 1]

    @pl.when(step == 0)
    def _():
        for k, ref in enumerate(block_refs):
            kv_ref[k] = ref[...]

    q = q_ref[...].reshape(rows, dim)
    lower = jnp.concatenate([lower_ref[...]] * routes, axis=0)
    place = jnp.concatenate([place_ref[...]] * routes, axis=0)

    def block(masked, at, carry):
        peak, total, accum = carry
        first = at * KEY_BLOCK
        slot = jnp.where(at % 2 == core, 0, half) + at // 2
        keys = kv_ref[slot, :, :dim]
        values = kv_ref[slot, :, dim:]
        scores = lax.dot_general(
            q, keys, (((1,), (1,)), ((), ())), preferred_element_type=jnp.float32
        )
        if masked:
            key_place = first + lax.broadcasted_iota(jnp.int32, (1, KEY_BLOCK), 1)
            allowed = (key_place >= lower) & (key_place <= place)
            scores = jnp.where(allowed, scores, MASKED)
        new_peak = jnp.maximum(peak, jnp.max(scores, axis=1, keepdims=True))
        shrink = jnp.exp2(peak - new_peak)
        expon = jnp.exp2(scores - new_peak)
        total = total * shrink + jnp.sum(expon, axis=1, keepdims=True)
        accum = accum * shrink + jnp.dot(
            expon.astype(jnp.bfloat16), values, preferred_element_type=jnp.float32
        )
        return new_peak, total, accum

    state = (
        jnp.full((rows, 1), MASKED, jnp.float32),
        jnp.zeros((rows, 1), jnp.float32),
        jnp.zeros((rows, dim), jnp.float32),
    )
    start, full, edge, stop = (bounds_ref[4 * step + k] for k in range(4))
    state = lax.fori_loop(start, full, lambda at, c: block(True, at, c), state)
    state = lax.fori_loop(full, edge, lambda at, c: block(False, at, c), state)
    state = lax.fori_loop(edge, stop, lambda at, c: block(True, at, c), state)
    out_ref[...] = (state[2] / state[1]).astype(jnp.bfloat16).reshape(routes, tokens, dim)


def attend(queries, lower, place, core, blocks):
    routes, tokens, dim = queries.shape
    steps = tokens // QUERY_BLOCK
    first_lower = lower.reshape(steps, QUERY_BLOCK)[:, 0]
    last_lower = lower.reshape(steps, QUERY_BLOCK)[:, -1]
    first_place = place.reshape(steps, QUERY_BLOCK)[:, 0]
    last_place = place.reshape(steps, QUERY_BLOCK)[:, -1]
    start = first_lower // KEY_BLOCK
    stop = last_place // KEY_BLOCK + 1
    full = jnp.clip((last_lower + KEY_BLOCK - 1) // KEY_BLOCK, start, stop)
    edge = jnp.clip((first_place + 1) // KEY_BLOCK, full, stop)
    bounds = jnp.concatenate([jnp.stack([start, full, edge, stop], axis=1).reshape(-1), core[None]])
    return pl.pallas_call(
        attend_body,
        grid_spec=pltpu.PrefetchScalarGridSpec(
            num_scalar_prefetch=1,
            grid=(steps,),
            in_specs=[
                pl.BlockSpec((routes, QUERY_BLOCK, dim), lambda i, b: (0, i, 0)),
                pl.BlockSpec((QUERY_BLOCK, 1), lambda i, b: (i, 0)),
                pl.BlockSpec((QUERY_BLOCK, 1), lambda i, b: (i, 0)),
            ]
            + [pl.BlockSpec(block.shape, lambda i, b: (0, 0)) for block in blocks],
            out_specs=pl.BlockSpec((routes, QUERY_BLOCK, dim), lambda i, b: (0, i, 0)),
            scratch_shapes=[pltpu.VMEM((len(blocks),) + blocks[0].shape, jnp.bfloat16)],
        ),
        out_shape=jax.ShapeDtypeStruct((routes, tokens, dim), jnp.bfloat16),
        cost_estimate=cost(
            2 * routes * tokens * tokens * len(blocks) * dim,
            routes * tokens * tokens * len(blocks) // 2,
            4 * len(blocks) * tokens * dim,
        ),
    )(bounds, queries, lower[:, None], place[:, None], *blocks)


def mix_body(at_ref, own_ref, peer_ref, gates_ref, *refs):
    pieces, out_ref, mix_ref = piece_refs(refs[:-2]), refs[-2], refs[-1]
    experts, rows, cols = pieces[0].shape
    routes = own_ref.shape[0]
    own_first = at_ref[0] == 0
    for h in range(2):
        attended = [
            jnp.where(own_first == (h == 0), own_ref[s], peer_ref[s]).astype(jnp.float32)
            for s in range(routes)
        ]
        for e in range(experts):
            value = sum(
                attended[s] * gates_ref[:, s * experts + e : s * experts + e + 1]
                for s in range(routes)
            )
            mix_ref[h, :, e * rows : (e + 1) * rows] = value.astype(jnp.bfloat16)
    for step in range(CHIPS_X):
        total = jnp.zeros((out_ref.shape[1], 2 * cols), jnp.float32)
        for h in range(2):
            weight = jnp.concatenate(
                [
                    pieces[(c * CHIPS_X + step) * 2 + h][...].reshape(experts * rows, cols)
                    for c in range(2)
                ],
                axis=1,
            )
            total = total + jnp.dot(mix_ref[h], weight, preferred_element_type=jnp.float32)
        for c in range(2):
            out_ref[at_ref[1 + c * CHIPS_X + step]] = total[:, c * cols : (c + 1) * cols].astype(
                jnp.bfloat16
            )


def mix_heads(at, own, peer, gates, blocks):
    routes, tokens, dim = own.shape
    experts, rows, cols = blocks[0].shape[1:]
    whole = lambda i, s: (0, 0, 0)
    return pl.pallas_call(
        mix_body,
        grid_spec=pltpu.PrefetchScalarGridSpec(
            num_scalar_prefetch=1,
            grid=(1,),
            in_specs=[
                pl.BlockSpec((routes, tokens, dim), whole),
                pl.BlockSpec((routes, tokens, dim), whole),
                pl.BlockSpec(gates.shape, lambda i, s: (0, 0)),
            ]
            + [pl.BlockSpec(block.shape, lambda i, s: (0, 0, 0, 0)) for block in blocks],
            out_specs=pl.BlockSpec((2 * CHIPS_X, tokens, cols), whole),
            scratch_shapes=[pltpu.VMEM((2, tokens, experts * rows), jnp.bfloat16)],
        ),
        out_shape=jax.ShapeDtypeStruct((2 * CHIPS_X, tokens, cols), jnp.bfloat16),
        cost_estimate=cost(
            4 * tokens * experts * rows * 2 * CHIPS_X * cols, 0, 32 * blocks[0].size
        ),
    )(at, own, peer, gates, *blocks)


def local(
    hidden,
    segment_ids,
    routes,
    norm_gain,
    router_weight,
    query_weight,
    kv_weight,
    out_weight,
    page_table,
):
    tok_dev, width = hidden.shape
    experts, chunk, head_cols = query_weight.shape
    shards = lax.axis_size("tok")
    groups = lax.axis_size("mdl")
    half_tok, half_mdl = shards // 2, groups // 2
    tok_row = lax.axis_index("tok")
    mdl_row = lax.axis_index("mdl")
    core = tok_row % 2
    side = mdl_row // half_mdl

    core_swap = [(i, i ^ 1) for i in range(shards)]

    def along_x(block, sign):
        moves = []
        for i in range(shards):
            chip = (i // 2 % CHIPS_X + sign * (1 - i % 2 * 2)) % CHIPS_X
            moves.append((i, i // half_tok * half_tok + chip * 2 + i % 2))
        return lax.ppermute(block, "tok", moves)

    def both_cores(blocks):
        return blocks + [lax.ppermute(block, "tok", core_swap) for block in blocks]

    other_row = lax.ppermute(
        query_weight, "tok", [(i, (i + half_tok) % shards) for i in range(shards)]
    )

    pages_here = page_table.shape[0]
    labels = jnp.stack([page_table // pages_here, page_table % pages_here]).astype(jnp.bfloat16)
    piece = jnp.concatenate(
        [
            kv_weight.reshape(-1, head_cols),
            jnp.pad(labels, ((0, LABEL_ROWS - 2), (0, head_cols - pages_here))),
        ],
        axis=0,
    )
    same_core = [[2 * k + c for k in range(half_tok)] for c in range(2)]
    kv_mine = lax.all_to_all(
        jnp.broadcast_to(piece[None], (half_tok,) + piece.shape),
        "tok", 0, 0, axis_index_groups=same_core, tiled=True,
    )
    kv_other = lax.ppermute(kv_mine, "tok", core_swap)
    normed = rms_norm(hidden, norm_gain)
    query_own, _ = lax.optimization_barrier((jnp.stack([query_weight, other_row]), kv_mine))
    query_near, query_next = along_x(query_own, 1), along_x(query_own, -1)
    key_values = project_kv(core, normed, kv_mine, kv_other)

    near, _ = lax.optimization_barrier((query_near, key_values))
    query_far = along_x(near, 1)

    earlier = [
        lax.ppermute(key_values, "tok", [(i, i + 2 * s) for i in range(shards - 2 * s)])
        for s in range(WINDOW_PAIRS - 1, 0, -1)
    ]
    page = tok_dev // pages_here
    per_peer = pages_here // shards
    page_ids = jnp.arange(pages_here, dtype=jnp.int32)
    before = page_ids[:, None] > page_ids[None, :]
    targets = page_table // pages_here
    rank = jnp.sum(((targets[:, None] == targets[None, :]) & before).astype(jnp.int32), axis=1)
    slot = targets * per_peer + rank
    listing = jnp.sum(jnp.where(slot[None, :] == page_ids[:, None], page_ids[None, :], 0), axis=1)
    outgoing = key_values.reshape(pages_here, page, 2 * head_cols)[listing]
    incoming = lax.all_to_all(outgoing, "tok", 0, 0, tiled=True)
    got = jnp.concatenate([kv_mine, kv_other])[:, 2 * CHUNK : 2 * CHUNK + 2, :pages_here]
    chips = jnp.arange(half_tok, dtype=jnp.int32) * 2
    senders = jnp.concatenate([chips + core, chips + 1 - core])
    target = got[:, 0] == tok_row.astype(jnp.bfloat16)
    order = jnp.sum((target[:, None, :] & before[None]).astype(jnp.int32), axis=2)
    chosen = target[None] & (got[None, :, 1] == page_ids.astype(jnp.bfloat16)[:, None, None])
    source = jnp.sum(jnp.where(chosen, (senders[:, None] * per_peer + order)[None], 0), axis=(1, 2))

    out_early, _ = lax.optimization_barrier((out_weight, kv_mine))

    def along_y(step):
        moves = []
        for a in range(2):
            for b in range(2):
                for i in range(half_tok):
                    for z in range(half_mdl):
                        source = (a * half_tok + i) * groups + (b ^ step) * half_mdl + z
                        moves.append((source, (b * half_tok + i) * groups + a * half_mdl + z))
        return lax.ppermute(out_early, ("tok", "mdl"), moves)

    out_own = jnp.stack([along_y(0), along_y(1)])
    earlier, query_near, query_next, query_far, out_own, incoming, late_normed = (
        lax.optimization_barrier(
            (earlier, query_near, query_next, query_far, out_own, incoming, normed)
        )
    )
    mine = earlier + [key_values]
    window = mine + [lax.ppermute(block, "tok", core_swap) for block in mine]

    query_blocks = both_cores([query_own, query_near, query_next, query_far])
    out_near, out_next = along_x(out_own, 1), along_x(out_own, -1)

    window_first = (tok_row // 2 - (WINDOW_PAIRS - 1)) * 2 * tok_dev
    own_first = tok_row * tok_dev
    own_segments = lax.dynamic_slice_in_dim(segment_ids, own_first, tok_dev)
    prompt_ids = jnp.arange(SEGS, dtype=jnp.int32)
    seg_first = jnp.sum((segment_ids[:, None] < prompt_ids[None, :]).astype(jnp.int32), axis=0)
    lower = jnp.sum(
        jnp.where(own_segments[:, None] == prompt_ids[None, :], seg_first[None, :], 0), axis=1
    )
    place = own_first + jnp.arange(tok_dev, dtype=jnp.int32)
    gates = route_weights(late_normed, router_weight, routes)

    owners = owners_of(tok_row, half_tok)
    queries = project_queries(jnp.stack(owners), normed, query_blocks, routes)
    queries, out_near, out_next = lax.optimization_barrier((queries, out_near, out_next))
    out_blocks = both_cores([out_own, out_near, out_next, along_x(out_near, 1)])
    attended = attend(queries, lower - window_first, place - window_first, core, window)
    peer = lax.ppermute(attended, "mdl", [(j, j ^ half_mdl) for j in range(groups)])
    chunk_at = [owner % half_tok for owner in owners[::2]]
    at = jnp.stack([tok_row // half_tok ^ side] + chunk_at)
    partial_sums = mix_heads(at, attended, peer, gates, out_blocks)
    sides = [[b * half_mdl + z for z in range(half_mdl)] for b in range(2)]
    arrived = lax.all_to_all(partial_sums, "mdl", 0, 0, axis_index_groups=sides, tiled=True)
    mixed = jnp.sum(arrived.astype(jnp.float32), axis=0)
    span = width // groups
    residual = lax.dynamic_slice_in_dim(hidden, mdl_row * span, span, 1)
    output = (residual.astype(jnp.float32) + mixed).astype(jnp.bfloat16)

    cache = incoming[source].reshape(pages_here, page, 2, head_cols)
    return (output, cache)


def solution(mesh):
    placed = (
        P("tok", None),
        P(),
        P("tok", None),
        P(),
        P(),
        P(None, "tok", "mdl"),
        P(None, "tok", "mdl"),
        P(None, "mdl", "tok"),
        P("tok"),
    )
    return jax.shard_map(
        local,
        mesh=mesh,
        in_specs=placed,
        out_specs=(P("tok", "mdl"), P("tok", None, None, "mdl")),
        check_vma=False,
    )
```

```python
import math

import jax
import jax.numpy as jnp
from jax import lax
from jax.experimental import pallas as pl
from jax.experimental.pallas import tpu as pltpu
from jax.sharding import PartitionSpec as P

HDIM = 128
CHUNK = 128
LABEL_ROWS = 16
CHIPS_X = 4
WINDOW_PAIRS = 5
SEGS = 4
EPSILON = 1e-05
MASKED = -1e30
KEY_BLOCK = 512
QUERY_BLOCK = 256
QUERY_SCALE = math.log2(math.e) / math.sqrt(HDIM)


def rms_norm(hidden, norm_gain):
    values = hidden.astype(jnp.float32)
    factor = lax.rsqrt(jnp.mean(values * values, axis=-1, keepdims=True) + EPSILON)
    return (values * factor * norm_gain).astype(jnp.bfloat16)


def route_weights(normed, router_weight, routes):
    logits = jnp.dot(normed.astype(jnp.float32), router_weight, precision=lax.Precision.HIGHEST)
    expert_ids = jnp.arange(logits.shape[1], dtype=jnp.int32)
    picked = routes[:, :, None] == expert_ids[None, None, :]
    chosen = jnp.sum(jnp.where(picked, logits[:, None, :], jnp.float32(0.0)), axis=-1)
    gates = jax.nn.softmax(chosen, axis=-1)
    return jnp.where(picked, gates[:, :, None], 0.0).reshape(routes.shape[0], -1)


def cost(flops, transcendentals, moved):
    return pl.CostEstimate(flops=flops, transcendentals=transcendentals, bytes_accessed=moved)


def kv_body(core_ref, normed_ref, mine_ref, other_ref, out_ref, weight_ref):
    @pl.when(pl.program_id(0) == 0)
    def _():
        first = core_ref[0] == 0
        for k in range(mine_ref.shape[0]):
            for m in range(2):
                at = slice(m * CHUNK, (m + 1) * CHUNK)
                mine, other = mine_ref[k, at], other_ref[k, at]
                row = 2 * k * CHUNK
                weight_ref[row : row + CHUNK, at] = jnp.where(first, mine, other)
                weight_ref[row + CHUNK : row + 2 * CHUNK, at] = jnp.where(first, other, mine)

    total = jnp.dot(normed_ref[...], weight_ref[...], preferred_element_type=jnp.float32)
    out_ref[...] = total.astype(jnp.bfloat16)


def project_kv(core, normed, mine, other):
    tokens, width = normed.shape
    chips, _, cols = mine.shape
    rows = tokens // 2
    whole = pl.BlockSpec((chips, 2 * CHUNK, cols), lambda i, c: (0, 0, 0))
    return pl.pallas_call(
        kv_body,
        grid_spec=pltpu.PrefetchScalarGridSpec(
            num_scalar_prefetch=1,
            grid=(2,),
            in_specs=[pl.BlockSpec((rows, width), lambda i, c: (i, 0)), whole, whole],
            out_specs=pl.BlockSpec((rows, 2 * cols), lambda i, c: (i, 0)),
            scratch_shapes=[pltpu.VMEM((width, 2 * cols), jnp.bfloat16)],
        ),
        out_shape=jax.ShapeDtypeStruct((tokens, 2 * cols), jnp.bfloat16),
        cost_estimate=cost(2 * tokens * width * 2 * cols, 0, 2 * tokens * width),
    )(core[None], normed, mine, other)


def owners_of(tok_row, half_tok):
    core, chip, row = tok_row % 2, tok_row // 2 % CHIPS_X, tok_row // half_tok
    owners = []
    for c in range(2):
        source = core ^ c
        for step in (0, 2 * source - 1, 1 - 2 * source, 2):
            at = (chip + CHIPS_X + step) % CHIPS_X * 2 + source
            owners += [(row ^ r) * half_tok + at for r in range(2)]
    return owners


def piece_refs(refs):
    return [ref.at[row] for ref in refs for row in range(2)]


def query_body(owner_ref, normed_ref, routes_ref, *refs):
    pieces, out_ref, ordered_ref = piece_refs(refs[:-2]), refs[-2], refs[-1]
    step = pl.program_id(0)
    pair = pieces[0].shape[0]
    cols = out_ref.shape[2]

    @pl.when(step == 0)
    def _():
        for k in range(len(pieces)):
            at = pl.ds(pl.multiple_of(owner_ref[k] * CHUNK, CHUNK), CHUNK)
            ordered_ref[:, k * CHUNK : (k + 1) * CHUNK] = normed_ref[:, at]

    weights = [jnp.concatenate([ref[k] for ref in pieces], axis=0) for k in range(pair)]
    total = jnp.dot(
        ordered_ref[...], jnp.concatenate(weights, axis=1), preferred_element_type=jnp.float32
    )
    for s in range(out_ref.shape[0]):
        route = routes_ref[:, s : s + 1]
        value = out_ref[s]
        for k in range(pair):
            mine = (total[:, k * cols : (k + 1) * cols] * QUERY_SCALE).astype(jnp.bfloat16)
            value = jnp.where(route == step * pair + k, mine, value)
        out_ref[s] = value


def project_queries(owners, normed, blocks, routes):
    tokens, width = normed.shape
    experts, rows, cols = blocks[0].shape[1:]
    return pl.pallas_call(
        query_body,
        grid_spec=pltpu.PrefetchScalarGridSpec(
            num_scalar_prefetch=1,
            grid=(experts // 2,),
            in_specs=[
                pl.BlockSpec((tokens, width), lambda e, r: (0, 0)),
                pl.BlockSpec(routes.shape, lambda e, r: (0, 0)),
            ]
            + [
                pl.BlockSpec((2, 2, rows, cols), lambda e, r: (0, e, 0, 0))
                for _ in blocks
            ],
            out_specs=pl.BlockSpec((routes.shape[1], tokens, cols), lambda e, r: (0, 0, 0)),
            scratch_shapes=[pltpu.VMEM((tokens, width), jnp.bfloat16)],
        ),
        out_shape=jax.ShapeDtypeStruct((routes.shape[1], tokens, cols), jnp.bfloat16),
        cost_estimate=cost(2 * tokens * width * experts * cols, 0, 4 * normed.size),
    )(owners, normed, routes, *blocks)


def attend_body(bounds_ref, q_ref, lower_ref, place_ref, *refs):
    block_refs, out_ref, kv_ref = refs[:-2], refs[-2], refs[-1]
    step = pl.program_id(0)
    routes, tokens, dim = q_ref.shape
    rows = routes * tokens
    half = len(block_refs) // 2
    core = bounds_ref[bounds_ref.shape[0] - 1]

    @pl.when(step == 0)
    def _():
        for k, ref in enumerate(block_refs):
            kv_ref[k] = ref[...]

    q = q_ref[...].reshape(rows, dim)
    lower = jnp.concatenate([lower_ref[...]] * routes, axis=0)
    place = jnp.concatenate([place_ref[...]] * routes, axis=0)

    def block(masked, at, carry):
        peak, total, accum = carry
        first = at * KEY_BLOCK
        slot = jnp.where(at % 2 == core, 0, half) + at // 2
        keys = kv_ref[slot, :, :dim]
        values = kv_ref[slot, :, dim:]
        scores = lax.dot_general(
            q, keys, (((1,), (1,)), ((), ())), preferred_element_type=jnp.float32
        )
        if masked:
            key_place = first + lax.broadcasted_iota(jnp.int32, (1, KEY_BLOCK), 1)
            allowed = (key_place >= lower) & (key_place <= place)
            scores = jnp.where(allowed, scores, MASKED)
        new_peak = jnp.maximum(peak, jnp.max(scores, axis=1, keepdims=True))
        shrink = jnp.exp2(peak - new_peak)
        expon = jnp.exp2(scores - new_peak)
        total = total * shrink + jnp.sum(expon, axis=1, keepdims=True)
        accum = accum * shrink + jnp.dot(
            expon.astype(jnp.bfloat16), values, preferred_element_type=jnp.float32
        )
        return new_peak, total, accum

    state = (
        jnp.full((rows, 1), MASKED, jnp.float32),
        jnp.zeros((rows, 1), jnp.float32),
        jnp.zeros((rows, dim), jnp.float32),
    )
    start, full, edge, stop = (bounds_ref[4 * step + k] for k in range(4))
    state = lax.fori_loop(start, full, lambda at, c: block(True, at, c), state)
    state = lax.fori_loop(full, edge, lambda at, c: block(False, at, c), state)
    state = lax.fori_loop(edge, stop, lambda at, c: block(True, at, c), state)
    out_ref[...] = (state[2] / state[1]).astype(jnp.bfloat16).reshape(routes, tokens, dim)


def attend_tables(lower, place, core):
    steps = lower.shape[0] // QUERY_BLOCK
    first_lower = lower.reshape(steps, QUERY_BLOCK)[:, 0]
    last_lower = lower.reshape(steps, QUERY_BLOCK)[:, -1]
    first_place = place.reshape(steps, QUERY_BLOCK)[:, 0]
    last_place = place.reshape(steps, QUERY_BLOCK)[:, -1]
    start = first_lower // KEY_BLOCK
    stop = last_place // KEY_BLOCK + 1
    full = jnp.clip((last_lower + KEY_BLOCK - 1) // KEY_BLOCK, start, stop)
    edge = jnp.clip((first_place + 1) // KEY_BLOCK, full, stop)
    bounds = jnp.concatenate([jnp.stack([start, full, edge, stop], axis=1).reshape(-1), core[None]])
    return bounds, lower[:, None], place[:, None]


def attend(queries, tables, blocks):
    routes, tokens, dim = queries.shape
    steps = tokens // QUERY_BLOCK
    bounds, lower, place = tables
    return pl.pallas_call(
        attend_body,
        grid_spec=pltpu.PrefetchScalarGridSpec(
            num_scalar_prefetch=1,
            grid=(steps,),
            in_specs=[
                pl.BlockSpec((routes, QUERY_BLOCK, dim), lambda i, b: (0, i, 0)),
                pl.BlockSpec((QUERY_BLOCK, 1), lambda i, b: (i, 0)),
                pl.BlockSpec((QUERY_BLOCK, 1), lambda i, b: (i, 0)),
            ]
            + [pl.BlockSpec(block.shape, lambda i, b: (0, 0)) for block in blocks],
            out_specs=pl.BlockSpec((routes, QUERY_BLOCK, dim), lambda i, b: (0, i, 0)),
            scratch_shapes=[pltpu.VMEM((len(blocks),) + blocks[0].shape, jnp.bfloat16)],
        ),
        out_shape=jax.ShapeDtypeStruct((routes, tokens, dim), jnp.bfloat16),
        cost_estimate=cost(
            2 * routes * tokens * tokens * len(blocks) * dim,
            routes * tokens * tokens * len(blocks) // 2,
            4 * len(blocks) * tokens * dim,
        ),
    )(bounds, queries, lower, place, *blocks)


def mix_body(at_ref, own_ref, peer_ref, gates_ref, *refs):
    pieces, out_ref, mix_ref = piece_refs(refs[:-2]), refs[-2], refs[-1]
    experts, rows, cols = pieces[0].shape
    routes = own_ref.shape[0]
    own_first = at_ref[0] == 0
    for h in range(2):
        attended = [
            jnp.where(own_first == (h == 0), own_ref[s], peer_ref[s]).astype(jnp.float32)
            for s in range(routes)
        ]
        for e in range(experts):
            value = sum(
                attended[s] * gates_ref[:, s * experts + e : s * experts + e + 1]
                for s in range(routes)
            )
            mix_ref[h, :, e * rows : (e + 1) * rows] = value.astype(jnp.bfloat16)
    for step in range(CHIPS_X):
        total = jnp.zeros((out_ref.shape[1], 2 * cols), jnp.float32)
        for h in range(2):
            weight = jnp.concatenate(
                [
                    pieces[(c * CHIPS_X + step) * 2 + h][...].reshape(experts * rows, cols)
                    for c in range(2)
                ],
                axis=1,
            )
            total = total + jnp.dot(mix_ref[h], weight, preferred_element_type=jnp.float32)
        for c in range(2):
            out_ref[at_ref[1 + c * CHIPS_X + step]] = total[:, c * cols : (c + 1) * cols].astype(
                jnp.bfloat16
            )


def mix_heads(at, own, peer, gates, blocks):
    routes, tokens, dim = own.shape
    experts, rows, cols = blocks[0].shape[1:]
    whole = lambda i, s: (0, 0, 0)
    return pl.pallas_call(
        mix_body,
        grid_spec=pltpu.PrefetchScalarGridSpec(
            num_scalar_prefetch=1,
            grid=(1,),
            in_specs=[
                pl.BlockSpec((routes, tokens, dim), whole),
                pl.BlockSpec((routes, tokens, dim), whole),
                pl.BlockSpec(gates.shape, lambda i, s: (0, 0)),
            ]
            + [pl.BlockSpec(block.shape, lambda i, s: (0, 0, 0, 0)) for block in blocks],
            out_specs=pl.BlockSpec((2 * CHIPS_X, tokens, cols), whole),
            scratch_shapes=[pltpu.VMEM((2, tokens, experts * rows), jnp.bfloat16)],
        ),
        out_shape=jax.ShapeDtypeStruct((2 * CHIPS_X, tokens, cols), jnp.bfloat16),
        cost_estimate=cost(
            4 * tokens * experts * rows * 2 * CHIPS_X * cols, 0, 32 * blocks[0].size
        ),
    )(at, own, peer, gates, *blocks)


def local(
    hidden,
    segment_ids,
    routes,
    norm_gain,
    router_weight,
    query_weight,
    kv_weight,
    out_weight,
    page_table,
):
    tok_dev, width = hidden.shape
    experts, chunk, head_cols = query_weight.shape
    shards = lax.axis_size("tok")
    groups = lax.axis_size("mdl")
    half_tok, half_mdl = shards // 2, groups // 2
    tok_row = lax.axis_index("tok")
    mdl_row = lax.axis_index("mdl")
    core = tok_row % 2
    side = mdl_row // half_mdl

    core_swap = [(i, i ^ 1) for i in range(shards)]

    def along_x(block, sign):
        moves = []
        for i in range(shards):
            chip = (i // 2 % CHIPS_X + sign * (1 - i % 2 * 2)) % CHIPS_X
            moves.append((i, i // half_tok * half_tok + chip * 2 + i % 2))
        return lax.ppermute(block, "tok", moves)

    def both_cores(blocks):
        return blocks + [lax.ppermute(block, "tok", core_swap) for block in blocks]

    other_row = lax.ppermute(
        query_weight, "tok", [(i, (i + half_tok) % shards) for i in range(shards)]
    )

    pages_here = page_table.shape[0]
    labels = jnp.stack([page_table // pages_here, page_table % pages_here]).astype(jnp.bfloat16)
    piece = jnp.concatenate(
        [
            kv_weight.reshape(-1, head_cols),
            jnp.pad(labels, ((0, LABEL_ROWS - 2), (0, head_cols - pages_here))),
        ],
        axis=0,
    )
    same_core = [[2 * k + c for k in range(half_tok)] for c in range(2)]
    kv_mine = lax.all_to_all(
        jnp.broadcast_to(piece[None], (half_tok,) + piece.shape),
        "tok", 0, 0, axis_index_groups=same_core, tiled=True,
    )
    kv_other = lax.ppermute(kv_mine, "tok", core_swap)
    normed = rms_norm(hidden, norm_gain)
    query_own, _ = lax.optimization_barrier((jnp.stack([query_weight, other_row]), kv_mine))
    query_near, query_next = along_x(query_own, 1), along_x(query_own, -1)
    key_values = project_kv(core, normed, kv_mine, kv_other)

    near, _ = lax.optimization_barrier((query_near, key_values))
    query_far = along_x(near, 1)

    earlier = [
        lax.ppermute(key_values, "tok", [(i, i + 2 * s) for i in range(shards - 2 * s)])
        for s in range(WINDOW_PAIRS - 1, 0, -1)
    ]
    page = tok_dev // pages_here
    per_peer = pages_here // shards
    page_ids = jnp.arange(pages_here, dtype=jnp.int32)
    before = page_ids[:, None] > page_ids[None, :]
    targets = page_table // pages_here
    rank = jnp.sum(((targets[:, None] == targets[None, :]) & before).astype(jnp.int32), axis=1)
    slot = targets * per_peer + rank
    listing = jnp.sum(jnp.where(slot[None, :] == page_ids[:, None], page_ids[None, :], 0), axis=1)
    outgoing = key_values.reshape(pages_here, page, 2 * head_cols)[listing]
    incoming = lax.all_to_all(outgoing, "tok", 0, 0, tiled=True)
    got = jnp.concatenate([kv_mine, kv_other])[:, 2 * CHUNK : 2 * CHUNK + 2, :pages_here]
    chips = jnp.arange(half_tok, dtype=jnp.int32) * 2
    senders = jnp.concatenate([chips + core, chips + 1 - core])
    target = got[:, 0] == tok_row.astype(jnp.bfloat16)
    order = jnp.sum((target[:, None, :] & before[None]).astype(jnp.int32), axis=2)
    chosen = target[None] & (got[None, :, 1] == page_ids.astype(jnp.bfloat16)[:, None, None])
    source = jnp.sum(jnp.where(chosen, (senders[:, None] * per_peer + order)[None], 0), axis=(1, 2))

    out_early, _ = lax.optimization_barrier((out_weight, kv_mine))

    def along_y(step):
        moves = []
        for a in range(2):
            for b in range(2):
                for i in range(half_tok):
                    for z in range(half_mdl):
                        source = (a * half_tok + i) * groups + (b ^ step) * half_mdl + z
                        moves.append((source, (b * half_tok + i) * groups + a * half_mdl + z))
        return lax.ppermute(out_early, ("tok", "mdl"), moves)

    out_own = jnp.stack(lax.optimization_barrier((along_y(0), along_y(1), key_values))[:2])
    late_ids, late_normed, late_row, _ = lax.optimization_barrier(
        (segment_ids, normed, tok_row, key_values)
    )
    window_first = (late_row // 2 - (WINDOW_PAIRS - 1)) * 2 * tok_dev
    own_first = late_row * tok_dev
    own_segments = lax.dynamic_slice_in_dim(late_ids, own_first, tok_dev)
    prompt_ids = jnp.arange(SEGS, dtype=jnp.int32)
    seg_first = jnp.sum((late_ids[:, None] < prompt_ids[None, :]).astype(jnp.int32), axis=0)
    lower = jnp.sum(
        jnp.where(own_segments[:, None] == prompt_ids[None, :], seg_first[None, :], 0), axis=1
    )
    place = own_first + jnp.arange(tok_dev, dtype=jnp.int32)
    tables = attend_tables(lower - window_first, place - window_first, late_row % 2)
    gates = route_weights(late_normed, router_weight, routes)
    owners = owners_of(late_row, half_tok)
    chunk_at = [owner % half_tok for owner in owners[::2]]
    at = jnp.stack([late_row // half_tok ^ side] + chunk_at)
    owners = jnp.stack(owners)
    (earlier, query_near, query_next, query_far, out_own, incoming, tables, gates, at, owners) = (
        lax.optimization_barrier(
            (earlier, query_near, query_next, query_far, out_own, incoming, tables, gates, at, owners)
        )
    )
    mine = earlier + [key_values]
    window = mine + [lax.ppermute(block, "tok", core_swap) for block in mine]

    query_blocks = both_cores([query_own, query_near, query_next, query_far])
    out_near, out_next = along_x(out_own, 1), along_x(out_own, -1)

    queries = project_queries(owners, normed, query_blocks, routes)
    queries, out_near, out_next = lax.optimization_barrier((queries, out_near, out_next))
    out_far = along_x(out_near, 1)
    attended = attend(queries, tables, window)
    attended, out_far = lax.optimization_barrier((attended, out_far))
    out_blocks = both_cores([out_own, out_near, out_next, out_far])
    peer = lax.ppermute(attended, "mdl", [(j, j ^ half_mdl) for j in range(groups)])
    partial_sums = mix_heads(at, attended, peer, gates, out_blocks)
    sides = [[b * half_mdl + z for z in range(half_mdl)] for b in range(2)]
    arrived = lax.all_to_all(partial_sums, "mdl", 0, 0, axis_index_groups=sides, tiled=True)
    mixed = jnp.sum(arrived.astype(jnp.float32), axis=0)
    span = width // groups
    residual = lax.dynamic_slice_in_dim(hidden, mdl_row * span, span, 1)
    output = (residual.astype(jnp.float32) + mixed).astype(jnp.bfloat16)

    cache = incoming[source].reshape(pages_here, page, 2, head_cols)
    return (output, cache)


def solution(mesh):
    placed = (
        P("tok", None),
        P(),
        P("tok", None),
        P(),
        P(),
        P(None, "tok", "mdl"),
        P(None, "tok", "mdl"),
        P(None, "mdl", "tok"),
        P("tok"),
    )
    return jax.shard_map(
        local,
        mesh=mesh,
        in_specs=placed,
        out_specs=(P("tok", "mdl"), P("tok", None, None, "mdl")),
        check_vma=False,
    )
```

```python
import math

import jax
import jax.numpy as jnp
from jax import lax
from jax.experimental import pallas as pl
from jax.experimental.pallas import tpu as pltpu
from jax.sharding import PartitionSpec as P

HDIM = 128
CHUNK = 128
LABEL_ROWS = 16
CHIPS_X = 4
WINDOW_PAIRS = 5
SEGS = 4
EPSILON = 1e-05
MASKED = -1e30
KEY_BLOCK = 512
QUERY_BLOCK = 256
QUERY_SCALE = math.log2(math.e) / math.sqrt(HDIM)


def rms_norm(hidden, norm_gain):
    values = hidden.astype(jnp.float32)
    factor = lax.rsqrt(jnp.mean(values * values, axis=-1, keepdims=True) + EPSILON)
    return (values * factor * norm_gain).astype(jnp.bfloat16)


def route_weights(normed, router_weight, routes):
    logits = jnp.dot(normed.astype(jnp.float32), router_weight, precision=lax.Precision.HIGHEST)
    expert_ids = jnp.arange(logits.shape[1], dtype=jnp.int32)
    picked = routes[:, :, None] == expert_ids[None, None, :]
    chosen = jnp.sum(jnp.where(picked, logits[:, None, :], jnp.float32(0.0)), axis=-1)
    gates = jax.nn.softmax(chosen, axis=-1)
    return jnp.where(picked, gates[:, :, None], 0.0).reshape(routes.shape[0], -1)


def cost(flops, transcendentals, moved):
    return pl.CostEstimate(flops=flops, transcendentals=transcendentals, bytes_accessed=moved)


def kv_body(core_ref, normed_ref, mine_ref, other_ref, out_ref, weight_ref):
    @pl.when(pl.program_id(0) == 0)
    def _():
        first = core_ref[0] == 0
        for k in range(mine_ref.shape[0]):
            for m in range(2):
                at = slice(m * CHUNK, (m + 1) * CHUNK)
                mine, other = mine_ref[k, at], other_ref[k, at]
                row = 2 * k * CHUNK
                weight_ref[row : row + CHUNK, at] = jnp.where(first, mine, other)
                weight_ref[row + CHUNK : row + 2 * CHUNK, at] = jnp.where(first, other, mine)

    total = jnp.dot(normed_ref[...], weight_ref[...], preferred_element_type=jnp.float32)
    out_ref[...] = total.astype(jnp.bfloat16)


def project_kv(core, normed, mine, other):
    tokens, width = normed.shape
    chips, _, cols = mine.shape
    rows = tokens // 2
    whole = pl.BlockSpec((chips, 2 * CHUNK, cols), lambda i, c: (0, 0, 0))
    return pl.pallas_call(
        kv_body,
        grid_spec=pltpu.PrefetchScalarGridSpec(
            num_scalar_prefetch=1,
            grid=(2,),
            in_specs=[pl.BlockSpec((rows, width), lambda i, c: (i, 0)), whole, whole],
            out_specs=pl.BlockSpec((rows, 2 * cols), lambda i, c: (i, 0)),
            scratch_shapes=[pltpu.VMEM((width, 2 * cols), jnp.bfloat16)],
        ),
        out_shape=jax.ShapeDtypeStruct((tokens, 2 * cols), jnp.bfloat16),
        cost_estimate=cost(2 * tokens * width * 2 * cols, 0, 2 * tokens * width),
    )(core[None], normed, mine, other)


def owners_of(tok_row, half_tok):
    core, chip, row = tok_row % 2, tok_row // 2 % CHIPS_X, tok_row // half_tok
    owners = []
    for c in range(2):
        source = core ^ c
        for step in (0, 2 * source - 1, 1 - 2 * source, 2):
            at = (chip + CHIPS_X + step) % CHIPS_X * 2 + source
            owners += [(row ^ r) * half_tok + at for r in range(2)]
    return owners


def piece_refs(refs):
    return [ref.at[row] for ref in refs for row in range(2)]


def query_body(owner_ref, normed_ref, routes_ref, *refs):
    pieces, out_ref, ordered_ref = piece_refs(refs[:-2]), refs[-2], refs[-1]
    step = pl.program_id(0)
    pair = pieces[0].shape[0]
    cols = out_ref.shape[2]

    @pl.when(step == 0)
    def _():
        for k in range(len(pieces)):
            at = pl.ds(pl.multiple_of(owner_ref[k] * CHUNK, CHUNK), CHUNK)
            ordered_ref[:, k * CHUNK : (k + 1) * CHUNK] = normed_ref[:, at]

    weights = [jnp.concatenate([ref[k] for ref in pieces], axis=0) for k in range(pair)]
    total = jnp.dot(
        ordered_ref[...], jnp.concatenate(weights, axis=1), preferred_element_type=jnp.float32
    )
    for s in range(out_ref.shape[0]):
        route = routes_ref[:, s : s + 1]
        value = out_ref[s]
        for k in range(pair):
            mine = (total[:, k * cols : (k + 1) * cols] * QUERY_SCALE).astype(jnp.bfloat16)
            value = jnp.where(route == step * pair + k, mine, value)
        out_ref[s] = value


def project_queries(owners, normed, blocks, routes):
    tokens, width = normed.shape
    experts, rows, cols = blocks[0].shape[1:]
    return pl.pallas_call(
        query_body,
        grid_spec=pltpu.PrefetchScalarGridSpec(
            num_scalar_prefetch=1,
            grid=(experts // 2,),
            in_specs=[
                pl.BlockSpec((tokens, width), lambda e, r: (0, 0)),
                pl.BlockSpec(routes.shape, lambda e, r: (0, 0)),
            ]
            + [
                pl.BlockSpec((2, 2, rows, cols), lambda e, r: (0, e, 0, 0))
                for _ in blocks
            ],
            out_specs=pl.BlockSpec((routes.shape[1], tokens, cols), lambda e, r: (0, 0, 0)),
            scratch_shapes=[pltpu.VMEM((tokens, width), jnp.bfloat16)],
        ),
        out_shape=jax.ShapeDtypeStruct((routes.shape[1], tokens, cols), jnp.bfloat16),
        cost_estimate=cost(2 * tokens * width * experts * cols, 0, 4 * normed.size),
    )(owners, normed, routes, *blocks)


def attend_body(bounds_ref, q_ref, lower_ref, place_ref, *refs):
    block_refs, out_ref, kv_ref = refs[:-2], refs[-2], refs[-1]
    step = pl.program_id(0)
    routes, tokens, dim = q_ref.shape
    rows = routes * tokens
    half = len(block_refs) // 2
    core = bounds_ref[bounds_ref.shape[0] - 1]

    @pl.when(step == 0)
    def _():
        for k, ref in enumerate(block_refs):
            kv_ref[k] = ref[...]

    q = q_ref[...].reshape(rows, dim)
    lower = jnp.concatenate([lower_ref[...]] * routes, axis=0)
    place = jnp.concatenate([place_ref[...]] * routes, axis=0)

    def block(masked, at, carry):
        peak, total, accum = carry
        first = at * KEY_BLOCK
        slot = jnp.where(at % 2 == core, 0, half) + at // 2
        keys = kv_ref[slot, :, :dim]
        values = kv_ref[slot, :, dim:]
        scores = lax.dot_general(
            q, keys, (((1,), (1,)), ((), ())), preferred_element_type=jnp.float32
        )
        if masked:
            key_place = first + lax.broadcasted_iota(jnp.int32, (1, KEY_BLOCK), 1)
            allowed = (key_place >= lower) & (key_place <= place)
            scores = jnp.where(allowed, scores, MASKED)
        new_peak = jnp.maximum(peak, jnp.max(scores, axis=1, keepdims=True))
        shrink = jnp.exp2(peak - new_peak)
        expon = jnp.exp2(scores - new_peak)
        total = total * shrink + jnp.sum(expon, axis=1, keepdims=True)
        accum = accum * shrink + jnp.dot(
            expon.astype(jnp.bfloat16), values, preferred_element_type=jnp.float32
        )
        return new_peak, total, accum

    state = (
        jnp.full((rows, 1), MASKED, jnp.float32),
        jnp.zeros((rows, 1), jnp.float32),
        jnp.zeros((rows, dim), jnp.float32),
    )
    start, full, edge, stop = (bounds_ref[4 * step + k] for k in range(4))
    state = lax.fori_loop(start, full, lambda at, c: block(True, at, c), state)
    state = lax.fori_loop(full, edge, lambda at, c: block(False, at, c), state)
    state = lax.fori_loop(edge, stop, lambda at, c: block(True, at, c), state)
    out_ref[...] = (state[2] / state[1]).astype(jnp.bfloat16).reshape(routes, tokens, dim)


def attend(queries, lower, place, core, blocks):
    routes, tokens, dim = queries.shape
    steps = tokens // QUERY_BLOCK
    first_lower = lower.reshape(steps, QUERY_BLOCK)[:, 0]
    last_lower = lower.reshape(steps, QUERY_BLOCK)[:, -1]
    first_place = place.reshape(steps, QUERY_BLOCK)[:, 0]
    last_place = place.reshape(steps, QUERY_BLOCK)[:, -1]
    start = first_lower // KEY_BLOCK
    stop = last_place // KEY_BLOCK + 1
    full = jnp.clip((last_lower + KEY_BLOCK - 1) // KEY_BLOCK, start, stop)
    edge = jnp.clip((first_place + 1) // KEY_BLOCK, full, stop)
    bounds = jnp.concatenate([jnp.stack([start, full, edge, stop], axis=1).reshape(-1), core[None]])
    return pl.pallas_call(
        attend_body,
        grid_spec=pltpu.PrefetchScalarGridSpec(
            num_scalar_prefetch=1,
            grid=(steps,),
            in_specs=[
                pl.BlockSpec((routes, QUERY_BLOCK, dim), lambda i, b: (0, i, 0)),
                pl.BlockSpec((QUERY_BLOCK, 1), lambda i, b: (i, 0)),
                pl.BlockSpec((QUERY_BLOCK, 1), lambda i, b: (i, 0)),
            ]
            + [pl.BlockSpec(block.shape, lambda i, b: (0, 0)) for block in blocks],
            out_specs=pl.BlockSpec((routes, QUERY_BLOCK, dim), lambda i, b: (0, i, 0)),
            scratch_shapes=[pltpu.VMEM((len(blocks),) + blocks[0].shape, jnp.bfloat16)],
        ),
        out_shape=jax.ShapeDtypeStruct((routes, tokens, dim), jnp.bfloat16),
        cost_estimate=cost(
            2 * routes * tokens * tokens * len(blocks) * dim,
            routes * tokens * tokens * len(blocks) // 2,
            4 * len(blocks) * tokens * dim,
        ),
    )(bounds, queries, lower[:, None], place[:, None], *blocks)


def mix_body(at_ref, own_ref, peer_ref, gates_ref, *refs):
    pieces, out_ref, mix_ref = piece_refs(refs[:-2]), refs[-2], refs[-1]
    experts, rows, cols = pieces[0].shape
    routes = own_ref.shape[0]
    own_first = at_ref[0] == 0
    for h in range(2):
        attended = [
            jnp.where(own_first == (h == 0), own_ref[s], peer_ref[s]).astype(jnp.float32)
            for s in range(routes)
        ]
        for e in range(experts):
            value = sum(
                attended[s] * gates_ref[:, s * experts + e : s * experts + e + 1]
                for s in range(routes)
            )
            mix_ref[h, :, e * rows : (e + 1) * rows] = value.astype(jnp.bfloat16)
    for step in range(CHIPS_X):
        total = jnp.zeros((out_ref.shape[1], 2 * cols), jnp.float32)
        for h in range(2):
            weight = jnp.concatenate(
                [
                    pieces[(c * CHIPS_X + step) * 2 + h][...].reshape(experts * rows, cols)
                    for c in range(2)
                ],
                axis=1,
            )
            total = total + jnp.dot(mix_ref[h], weight, preferred_element_type=jnp.float32)
        for c in range(2):
            out_ref[at_ref[1 + c * CHIPS_X + step]] = total[:, c * cols : (c + 1) * cols].astype(
                jnp.bfloat16
            )


def mix_heads(at, own, peer, gates, blocks):
    routes, tokens, dim = own.shape
    experts, rows, cols = blocks[0].shape[1:]
    whole = lambda i, s: (0, 0, 0)
    return pl.pallas_call(
        mix_body,
        grid_spec=pltpu.PrefetchScalarGridSpec(
            num_scalar_prefetch=1,
            grid=(1,),
            in_specs=[
                pl.BlockSpec((routes, tokens, dim), whole),
                pl.BlockSpec((routes, tokens, dim), whole),
                pl.BlockSpec(gates.shape, lambda i, s: (0, 0)),
            ]
            + [pl.BlockSpec(block.shape, lambda i, s: (0, 0, 0, 0)) for block in blocks],
            out_specs=pl.BlockSpec((2 * CHIPS_X, tokens, cols), whole),
            scratch_shapes=[pltpu.VMEM((2, tokens, experts * rows), jnp.bfloat16)],
        ),
        out_shape=jax.ShapeDtypeStruct((2 * CHIPS_X, tokens, cols), jnp.bfloat16),
        cost_estimate=cost(
            4 * tokens * experts * rows * 2 * CHIPS_X * cols, 0, 32 * blocks[0].size
        ),
    )(at, own, peer, gates, *blocks)


def local(
    hidden,
    segment_ids,
    routes,
    norm_gain,
    router_weight,
    query_weight,
    kv_weight,
    out_weight,
    page_table,
):
    tok_dev, width = hidden.shape
    experts, chunk, head_cols = query_weight.shape
    shards = lax.axis_size("tok")
    groups = lax.axis_size("mdl")
    half_tok, half_mdl = shards // 2, groups // 2
    tok_row = lax.axis_index("tok")
    mdl_row = lax.axis_index("mdl")
    core = tok_row % 2
    side = mdl_row // half_mdl

    core_swap = [(i, i ^ 1) for i in range(shards)]

    def along_x(block, sign):
        moves = []
        for i in range(shards):
            chip = (i // 2 % CHIPS_X + sign * (1 - i % 2 * 2)) % CHIPS_X
            moves.append((i, i // half_tok * half_tok + chip * 2 + i % 2))
        return lax.ppermute(block, "tok", moves)

    def both_cores(blocks):
        return blocks + [lax.ppermute(block, "tok", core_swap) for block in blocks]

    other_row = lax.ppermute(
        query_weight, "tok", [(i, (i + half_tok) % shards) for i in range(shards)]
    )

    pages_here = page_table.shape[0]
    labels = jnp.stack([page_table // pages_here, page_table % pages_here]).astype(jnp.bfloat16)
    piece = jnp.concatenate(
        [
            kv_weight.reshape(-1, head_cols),
            jnp.pad(labels, ((0, LABEL_ROWS - 2), (0, head_cols - pages_here))),
        ],
        axis=0,
    )
    same_core = [[2 * k + c for k in range(half_tok)] for c in range(2)]
    kv_mine = lax.all_to_all(
        jnp.broadcast_to(piece[None], (half_tok,) + piece.shape),
        "tok", 0, 0, axis_index_groups=same_core, tiled=True,
    )
    kv_other = lax.ppermute(kv_mine, "tok", core_swap)
    normed = rms_norm(hidden, norm_gain)
    query_own, _ = lax.optimization_barrier((jnp.stack([query_weight, other_row]), kv_mine))
    query_near, query_next = along_x(query_own, 1), along_x(query_own, -1)
    key_values = project_kv(core, normed, kv_mine, kv_other)

    near, _ = lax.optimization_barrier((query_near, key_values))
    query_far = along_x(near, 1)

    earlier = [
        lax.ppermute(key_values, "tok", [(i, i + 2 * s) for i in range(shards - 2 * s)])
        for s in range(WINDOW_PAIRS - 1, 0, -1)
    ]
    page = tok_dev // pages_here
    per_peer = pages_here // shards
    page_ids = jnp.arange(pages_here, dtype=jnp.int32)
    before = page_ids[:, None] > page_ids[None, :]
    targets = page_table // pages_here
    rank = jnp.sum(((targets[:, None] == targets[None, :]) & before).astype(jnp.int32), axis=1)
    slot = targets * per_peer + rank
    listing = jnp.sum(jnp.where(slot[None, :] == page_ids[:, None], page_ids[None, :], 0), axis=1)
    outgoing = key_values.reshape(pages_here, page, 2 * head_cols)[listing]
    incoming = lax.all_to_all(outgoing, "tok", 0, 0, tiled=True)
    got = jnp.concatenate([kv_mine, kv_other])[:, 2 * CHUNK : 2 * CHUNK + 2, :pages_here]
    chips = jnp.arange(half_tok, dtype=jnp.int32) * 2
    senders = jnp.concatenate([chips + core, chips + 1 - core])
    target = got[:, 0] == tok_row.astype(jnp.bfloat16)
    order = jnp.sum((target[:, None, :] & before[None]).astype(jnp.int32), axis=2)
    chosen = target[None] & (got[None, :, 1] == page_ids.astype(jnp.bfloat16)[:, None, None])
    source = jnp.sum(jnp.where(chosen, (senders[:, None] * per_peer + order)[None], 0), axis=(1, 2))

    out_early, _ = lax.optimization_barrier((out_weight, kv_mine))

    def along_y(step):
        moves = []
        for a in range(2):
            for b in range(2):
                for i in range(half_tok):
                    for z in range(half_mdl):
                        source = (a * half_tok + i) * groups + (b ^ step) * half_mdl + z
                        moves.append((source, (b * half_tok + i) * groups + a * half_mdl + z))
        return lax.ppermute(out_early, ("tok", "mdl"), moves)

    out_own = jnp.stack([along_y(0), along_y(1)])
    earlier, query_near, query_next, query_far, out_own, incoming, late_normed = (
        lax.optimization_barrier(
            (earlier, query_near, query_next, query_far, out_own, incoming, normed)
        )
    )
    mine = earlier + [key_values]
    window = mine + [lax.ppermute(block, "tok", core_swap) for block in mine]

    query_blocks = both_cores([query_own, query_near, query_next, query_far])
    out_near, out_next = along_x(out_own, 1), along_x(out_own, -1)

    window_first = (tok_row // 2 - (WINDOW_PAIRS - 1)) * 2 * tok_dev
    own_first = tok_row * tok_dev
    own_segments = lax.dynamic_slice_in_dim(segment_ids, own_first, tok_dev)
    prompt_ids = jnp.arange(SEGS, dtype=jnp.int32)
    seg_first = jnp.sum((segment_ids[:, None] < prompt_ids[None, :]).astype(jnp.int32), axis=0)
    lower = jnp.sum(
        jnp.where(own_segments[:, None] == prompt_ids[None, :], seg_first[None, :], 0), axis=1
    )
    place = own_first + jnp.arange(tok_dev, dtype=jnp.int32)

    owners = owners_of(tok_row, half_tok)
    queries = project_queries(jnp.stack(owners), normed, query_blocks, routes)
    queries, out_near, out_next = lax.optimization_barrier((queries, out_near, out_next))
    out_far = along_x(out_near, 1)
    attended = attend(queries, lower - window_first, place - window_first, core, window)
    attended, out_far, late_normed = lax.optimization_barrier((attended, out_far, late_normed))
    gates = route_weights(late_normed, router_weight, routes)
    out_blocks = both_cores([out_own, out_near, out_next, out_far])
    peer = lax.ppermute(attended, "mdl", [(j, j ^ half_mdl) for j in range(groups)])
    chunk_at = [owner % half_tok for owner in owners[::2]]
    at = jnp.stack([tok_row // half_tok ^ side] + chunk_at)
    partial_sums = mix_heads(at, attended, peer, gates, out_blocks)
    sides = [[b * half_mdl + z for z in range(half_mdl)] for b in range(2)]
    arrived = lax.all_to_all(partial_sums, "mdl", 0, 0, axis_index_groups=sides, tiled=True)
    mixed = jnp.sum(arrived.astype(jnp.float32), axis=0)
    span = width // groups
    residual = lax.dynamic_slice_in_dim(hidden, mdl_row * span, span, 1)
    output = (residual.astype(jnp.float32) + mixed).astype(jnp.bfloat16)

    cache = incoming[source].reshape(pages_here, page, 2, head_cols)
    return (output, cache)


def solution(mesh):
    placed = (
        P("tok", None),
        P(),
        P("tok", None),
        P(),
        P(),
        P(None, "tok", "mdl"),
        P(None, "tok", "mdl"),
        P(None, "mdl", "tok"),
        P("tok"),
    )
    return jax.shard_map(
        local,
        mesh=mesh,
        in_specs=placed,
        out_specs=(P("tok", "mdl"), P("tok", None, None, "mdl")),
        check_vma=False,
    )
```

```python
import functools
import math

import jax
import jax.numpy as jnp
from jax import lax
from jax.experimental import pallas as pl
from jax.experimental.pallas import tpu as pltpu
from jax.sharding import PartitionSpec as P

HDIM = 128
CHUNK = 128
LABEL_ROWS = 16
CHIPS_X = 4
WINDOW_PAIRS = 5
SEGS = 4
EPSILON = 1e-05
MASKED = -1e30
KEY_BLOCK = 512
QUERY_BLOCK = 256
QUERY_SCALE = math.log2(math.e) / math.sqrt(HDIM)


def rms_norm(hidden, norm_gain):
    values = hidden.astype(jnp.float32)
    factor = lax.rsqrt(jnp.mean(values * values, axis=-1, keepdims=True) + EPSILON)
    return (values * factor * norm_gain).astype(jnp.bfloat16)


def route_weights(normed, router_weight, routes):
    logits = jnp.dot(normed.astype(jnp.float32), router_weight, precision=lax.Precision.HIGHEST)
    expert_ids = jnp.arange(logits.shape[1], dtype=jnp.int32)
    picked = routes[:, :, None] == expert_ids[None, None, :]
    chosen = jnp.sum(jnp.where(picked, logits[:, None, :], jnp.float32(0.0)), axis=-1)
    gates = jax.nn.softmax(chosen, axis=-1)
    return jnp.where(picked, gates[:, :, None], 0.0).reshape(routes.shape[0], -1)


def cost(flops, transcendentals, moved):
    return pl.CostEstimate(flops=flops, transcendentals=transcendentals, bytes_accessed=moved)


def kv_body(core_ref, normed_ref, mine_ref, other_ref, out_ref, weight_ref):
    @pl.when(pl.program_id(0) == 0)
    def _():
        first = core_ref[0] == 0
        for k in range(mine_ref.shape[0]):
            for m in range(2):
                at = slice(m * CHUNK, (m + 1) * CHUNK)
                mine, other = mine_ref[k, at], other_ref[k, at]
                row = 2 * k * CHUNK
                weight_ref[row : row + CHUNK, at] = jnp.where(first, mine, other)
                weight_ref[row + CHUNK : row + 2 * CHUNK, at] = jnp.where(first, other, mine)

    total = jnp.dot(normed_ref[...], weight_ref[...], preferred_element_type=jnp.float32)
    out_ref[...] = total.astype(jnp.bfloat16)


def project_kv(core, normed, mine, other):
    tokens, width = normed.shape
    chips, _, cols = mine.shape
    rows = tokens // 2
    whole = pl.BlockSpec((chips, 2 * CHUNK, cols), lambda i, c: (0, 0, 0))
    return pl.pallas_call(
        kv_body,
        grid_spec=pltpu.PrefetchScalarGridSpec(
            num_scalar_prefetch=1,
            grid=(2,),
            in_specs=[pl.BlockSpec((rows, width), lambda i, c: (i, 0)), whole, whole],
            out_specs=pl.BlockSpec((rows, 2 * cols), lambda i, c: (i, 0)),
            scratch_shapes=[pltpu.VMEM((width, 2 * cols), jnp.bfloat16)],
        ),
        out_shape=jax.ShapeDtypeStruct((tokens, 2 * cols), jnp.bfloat16),
        cost_estimate=cost(2 * tokens * width * 2 * cols, 0, 2 * tokens * width),
    )(core[None], normed, mine, other)


def owners_of(tok_row, half_tok):
    core, chip, row = tok_row % 2, tok_row // 2 % CHIPS_X, tok_row // half_tok
    owners = []
    for c in range(2):
        source = core ^ c
        for step in (0, 2 * source - 1, 1 - 2 * source, 2):
            at = (chip + CHIPS_X + step) % CHIPS_X * 2 + source
            owners += [(row ^ r) * half_tok + at for r in range(2)]
    return owners


def piece_refs(refs):
    return [ref.at[row] for ref in refs for row in range(2)]


def query_body(owner_ref, normed_ref, routes_ref, *refs):
    pieces, out_ref, ordered_ref = piece_refs(refs[:-2]), refs[-2], refs[-1]
    step = pl.program_id(0)
    pair = pieces[0].shape[0]
    cols = out_ref.shape[2]

    @pl.when(step == 0)
    def _():
        for k in range(len(pieces)):
            at = pl.ds(pl.multiple_of(owner_ref[k] * CHUNK, CHUNK), CHUNK)
            ordered_ref[:, k * CHUNK : (k + 1) * CHUNK] = normed_ref[:, at]

    weights = [jnp.concatenate([ref[k] for ref in pieces], axis=0) for k in range(pair)]
    total = jnp.dot(
        ordered_ref[...], jnp.concatenate(weights, axis=1), preferred_element_type=jnp.float32
    )
    for s in range(out_ref.shape[0]):
        route = routes_ref[:, s : s + 1]
        value = out_ref[s]
        for k in range(pair):
            mine = (total[:, k * cols : (k + 1) * cols] * QUERY_SCALE).astype(jnp.bfloat16)
            value = jnp.where(route == step * pair + k, mine, value)
        out_ref[s] = value


def project_queries(owners, normed, blocks, routes):
    tokens, width = normed.shape
    experts, rows, cols = blocks[0].shape[1:]
    return pl.pallas_call(
        query_body,
        grid_spec=pltpu.PrefetchScalarGridSpec(
            num_scalar_prefetch=1,
            grid=(experts // 2,),
            in_specs=[
                pl.BlockSpec((tokens, width), lambda e, r: (0, 0)),
                pl.BlockSpec(routes.shape, lambda e, r: (0, 0)),
            ]
            + [
                pl.BlockSpec((2, 2, rows, cols), lambda e, r: (0, e, 0, 0))
                for _ in blocks
            ],
            out_specs=pl.BlockSpec((routes.shape[1], tokens, cols), lambda e, r: (0, 0, 0)),
            scratch_shapes=[pltpu.VMEM((tokens, width), jnp.bfloat16)],
        ),
        out_shape=jax.ShapeDtypeStruct((routes.shape[1], tokens, cols), jnp.bfloat16),
        cost_estimate=cost(2 * tokens * width * experts * cols, 0, 4 * normed.size),
    )(owners, normed, routes, *blocks)


def attend_body(bounds_ref, q_ref, lower_ref, place_ref, *refs):
    block_refs, out_ref, kv_ref = refs[:-2], refs[-2], refs[-1]
    step = pl.program_id(0)
    routes, tokens, dim = q_ref.shape
    rows = routes * tokens
    half = len(block_refs) // 2
    core = bounds_ref[bounds_ref.shape[0] - 1]

    @pl.when(step == 0)
    def _():
        for k, ref in enumerate(block_refs):
            kv_ref[k] = ref[...]

    q = q_ref[...].reshape(rows, dim)
    lower = jnp.concatenate([lower_ref[...]] * routes, axis=0)
    place = jnp.concatenate([place_ref[...]] * routes, axis=0)

    def block(masked, at, carry):
        peak, total, accum = carry
        first = at * KEY_BLOCK
        slot = jnp.where(at % 2 == core, 0, half) + at // 2
        keys = kv_ref[slot, :, :dim]
        values = kv_ref[slot, :, dim:]
        scores = lax.dot_general(
            q, keys, (((1,), (1,)), ((), ())), preferred_element_type=jnp.float32
        )
        if masked:
            key_place = first + lax.broadcasted_iota(jnp.int32, (1, KEY_BLOCK), 1)
            allowed = (key_place >= lower) & (key_place <= place)
            scores = jnp.where(allowed, scores, MASKED)
        new_peak = jnp.maximum(peak, jnp.max(scores, axis=1, keepdims=True))
        shrink = jnp.exp2(peak - new_peak)
        expon = jnp.exp2(scores - new_peak)
        total = total * shrink + jnp.sum(expon, axis=1, keepdims=True)
        accum = accum * shrink + jnp.dot(
            expon.astype(jnp.bfloat16), values, preferred_element_type=jnp.float32
        )
        return new_peak, total, accum

    state = (
        jnp.full((rows, 1), MASKED, jnp.float32),
        jnp.zeros((rows, 1), jnp.float32),
        jnp.zeros((rows, dim), jnp.float32),
    )
    start, full, edge, stop = (bounds_ref[4 * step + k] for k in range(4))
    state = lax.fori_loop(start, full, lambda at, c: block(True, at, c), state)
    state = lax.fori_loop(full, edge, lambda at, c: block(False, at, c), state)
    state = lax.fori_loop(edge, stop, lambda at, c: block(True, at, c), state)
    out_ref[...] = (state[2] / state[1]).astype(jnp.bfloat16).reshape(routes, tokens, dim)


def attend(queries, lower, place, core, blocks):
    routes, tokens, dim = queries.shape
    steps = tokens // QUERY_BLOCK
    first_lower = lower.reshape(steps, QUERY_BLOCK)[:, 0]
    last_lower = lower.reshape(steps, QUERY_BLOCK)[:, -1]
    first_place = place.reshape(steps, QUERY_BLOCK)[:, 0]
    last_place = place.reshape(steps, QUERY_BLOCK)[:, -1]
    start = first_lower // KEY_BLOCK
    stop = last_place // KEY_BLOCK + 1
    full = jnp.clip((last_lower + KEY_BLOCK - 1) // KEY_BLOCK, start, stop)
    edge = jnp.clip((first_place + 1) // KEY_BLOCK, full, stop)
    bounds = jnp.concatenate([jnp.stack([start, full, edge, stop], axis=1).reshape(-1), core[None]])
    return pl.pallas_call(
        attend_body,
        grid_spec=pltpu.PrefetchScalarGridSpec(
            num_scalar_prefetch=1,
            grid=(steps,),
            in_specs=[
                pl.BlockSpec((routes, QUERY_BLOCK, dim), lambda i, b: (0, i, 0)),
                pl.BlockSpec((QUERY_BLOCK, 1), lambda i, b: (i, 0)),
                pl.BlockSpec((QUERY_BLOCK, 1), lambda i, b: (i, 0)),
            ]
            + [pl.BlockSpec(block.shape, lambda i, b: (0, 0)) for block in blocks],
            out_specs=pl.BlockSpec((routes, QUERY_BLOCK, dim), lambda i, b: (0, i, 0)),
            scratch_shapes=[pltpu.VMEM((len(blocks),) + blocks[0].shape, jnp.bfloat16)],
        ),
        out_shape=jax.ShapeDtypeStruct((routes, tokens, dim), jnp.bfloat16),
        cost_estimate=cost(
            2 * routes * tokens * tokens * len(blocks) * dim,
            routes * tokens * tokens * len(blocks) // 2,
            4 * len(blocks) * tokens * dim,
        ),
    )(bounds, queries, lower[:, None], place[:, None], *blocks)


def mix_body(has_start, at_ref, head_ref, gates_ref, *refs):
    blocks, out_ref, mix_ref = refs[:8], refs[-2], refs[-1]
    start_ref = refs[8] if has_start else None
    _, experts, rows, cols = blocks[0].shape
    routes = head_ref.shape[0]
    attended = [head_ref[s].astype(jnp.float32) for s in range(routes)]
    for e in range(experts):
        value = sum(
            attended[s] * gates_ref[:, s * experts + e : s * experts + e + 1]
            for s in range(routes)
        )
        mix_ref[:, e * rows : (e + 1) * rows] = value.astype(jnp.bfloat16)
    for step in range(CHIPS_X):
        weight = jnp.concatenate(
            [blocks[c * CHIPS_X + step][0].reshape(experts * rows, cols) for c in range(2)], axis=1
        )
        total = jnp.dot(mix_ref[...], weight, preferred_element_type=jnp.float32)
        for c in range(2):
            k = c * CHIPS_X + step
            part = total[:, c * cols : (c + 1) * cols]
            if has_start:
                part = part + start_ref[k]
                out_ref[at_ref[1 + k]] = part.astype(out_ref.dtype)
            else:
                out_ref[k] = part


def mix_head(at, head, gates, blocks, start):
    routes, tokens, dim = head.shape
    experts, rows, cols = blocks[0].shape[1:]
    whole = lambda i, s: (0, 0, 0)
    shape = (2 * CHIPS_X, tokens, cols)
    extra = [] if start is None else [start]
    return pl.pallas_call(
        functools.partial(mix_body, start is not None),
        grid_spec=pltpu.PrefetchScalarGridSpec(
            num_scalar_prefetch=1,
            grid=(1,),
            in_specs=[
                pl.BlockSpec((routes, tokens, dim), whole),
                pl.BlockSpec(gates.shape, lambda i, s: (0, 0)),
            ]
            + [
                pl.BlockSpec((1, experts, rows, cols), lambda i, s: (s[0], 0, 0, 0))
                for _ in blocks
            ]
            + [pl.BlockSpec(shape, whole) for _ in extra],
            out_specs=pl.BlockSpec(shape, whole),
            scratch_shapes=[pltpu.VMEM((tokens, experts * rows), jnp.bfloat16)],
        ),
        out_shape=jax.ShapeDtypeStruct(shape, jnp.float32 if start is None else jnp.bfloat16),
        cost_estimate=cost(
            2 * tokens * experts * rows * 2 * CHIPS_X * cols, 0, 16 * blocks[0].size
        ),
    )(at, head, gates, *blocks, *extra)


def local(
    hidden,
    segment_ids,
    routes,
    norm_gain,
    router_weight,
    query_weight,
    kv_weight,
    out_weight,
    page_table,
):
    tok_dev, width = hidden.shape
    experts, chunk, head_cols = query_weight.shape
    shards = lax.axis_size("tok")
    groups = lax.axis_size("mdl")
    half_tok, half_mdl = shards // 2, groups // 2
    tok_row = lax.axis_index("tok")
    mdl_row = lax.axis_index("mdl")
    core = tok_row % 2
    side = mdl_row // half_mdl

    core_swap = [(i, i ^ 1) for i in range(shards)]

    def along_x(block, sign):
        moves = []
        for i in range(shards):
            chip = (i // 2 % CHIPS_X + sign * (1 - i % 2 * 2)) % CHIPS_X
            moves.append((i, i // half_tok * half_tok + chip * 2 + i % 2))
        return lax.ppermute(block, "tok", moves)

    def both_cores(blocks):
        return blocks + [lax.ppermute(block, "tok", core_swap) for block in blocks]

    other_row = lax.ppermute(
        query_weight, "tok", [(i, (i + half_tok) % shards) for i in range(shards)]
    )

    pages_here = page_table.shape[0]
    labels = jnp.stack([page_table // pages_here, page_table % pages_here]).astype(jnp.bfloat16)
    piece = jnp.concatenate(
        [
            kv_weight.reshape(-1, head_cols),
            jnp.pad(labels, ((0, LABEL_ROWS - 2), (0, head_cols - pages_here))),
        ],
        axis=0,
    )
    same_core = [[2 * k + c for k in range(half_tok)] for c in range(2)]
    kv_mine = lax.all_to_all(
        jnp.broadcast_to(piece[None], (half_tok,) + piece.shape),
        "tok", 0, 0, axis_index_groups=same_core, tiled=True,
    )
    kv_other = lax.ppermute(kv_mine, "tok", core_swap)
    normed = rms_norm(hidden, norm_gain)
    query_own, _ = lax.optimization_barrier((jnp.stack([query_weight, other_row]), kv_mine))
    query_near, query_next = along_x(query_own, 1), along_x(query_own, -1)
    key_values = project_kv(core, normed, kv_mine, kv_other)

    near, _ = lax.optimization_barrier((query_near, key_values))
    query_far = along_x(near, 1)

    earlier = [
        lax.ppermute(key_values, "tok", [(i, i + 2 * s) for i in range(shards - 2 * s)])
        for s in range(WINDOW_PAIRS - 1, 0, -1)
    ]
    page = tok_dev // pages_here
    per_peer = pages_here // shards
    page_ids = jnp.arange(pages_here, dtype=jnp.int32)
    before = page_ids[:, None] > page_ids[None, :]
    targets = page_table // pages_here
    rank = jnp.sum(((targets[:, None] == targets[None, :]) & before).astype(jnp.int32), axis=1)
    slot = targets * per_peer + rank
    listing = jnp.sum(jnp.where(slot[None, :] == page_ids[:, None], page_ids[None, :], 0), axis=1)
    outgoing = key_values.reshape(pages_here, page, 2 * head_cols)[listing]
    incoming = lax.all_to_all(outgoing, "tok", 0, 0, tiled=True)
    got = jnp.concatenate([kv_mine, kv_other])[:, 2 * CHUNK : 2 * CHUNK + 2, :pages_here]
    chips = jnp.arange(half_tok, dtype=jnp.int32) * 2
    senders = jnp.concatenate([chips + core, chips + 1 - core])
    target = got[:, 0] == tok_row.astype(jnp.bfloat16)
    order = jnp.sum((target[:, None, :] & before[None]).astype(jnp.int32), axis=2)
    chosen = target[None] & (got[None, :, 1] == page_ids.astype(jnp.bfloat16)[:, None, None])
    source = jnp.sum(jnp.where(chosen, (senders[:, None] * per_peer + order)[None], 0), axis=(1, 2))

    out_early, _ = lax.optimization_barrier((out_weight, kv_mine))

    def along_y(step):
        moves = []
        for a in range(2):
            for b in range(2):
                for i in range(half_tok):
                    for z in range(half_mdl):
                        source = (a * half_tok + i) * groups + (b ^ step) * half_mdl + z
                        moves.append((source, (b * half_tok + i) * groups + a * half_mdl + z))
        return lax.ppermute(out_early, ("tok", "mdl"), moves)

    out_own = jnp.stack([along_y(0), along_y(1)])
    earlier, query_near, query_next, query_far, out_own, incoming, late_normed = (
        lax.optimization_barrier(
            (earlier, query_near, query_next, query_far, out_own, incoming, normed)
        )
    )
    mine = earlier + [key_values]
    window = mine + [lax.ppermute(block, "tok", core_swap) for block in mine]

    query_blocks = both_cores([query_own, query_near, query_next, query_far])
    out_near, out_next = along_x(out_own, 1), along_x(out_own, -1)

    window_first = (tok_row // 2 - (WINDOW_PAIRS - 1)) * 2 * tok_dev
    own_first = tok_row * tok_dev
    own_segments = lax.dynamic_slice_in_dim(segment_ids, own_first, tok_dev)
    prompt_ids = jnp.arange(SEGS, dtype=jnp.int32)
    seg_first = jnp.sum((segment_ids[:, None] < prompt_ids[None, :]).astype(jnp.int32), axis=0)
    lower = jnp.sum(
        jnp.where(own_segments[:, None] == prompt_ids[None, :], seg_first[None, :], 0), axis=1
    )
    place = own_first + jnp.arange(tok_dev, dtype=jnp.int32)
    gates = route_weights(late_normed, router_weight, routes)

    owners = owners_of(tok_row, half_tok)
    queries = project_queries(jnp.stack(owners), normed, query_blocks, routes)
    queries, out_near, out_next = lax.optimization_barrier((queries, out_near, out_next))
    out_blocks = both_cores([out_own, out_near, out_next, along_x(out_near, 1)])
    attended = attend(queries, lower - window_first, place - window_first, core, window)
    peer = lax.ppermute(attended, "mdl", [(j, j ^ half_mdl) for j in range(groups)])
    chunk_at = [owner % half_tok for owner in owners[::2]]
    own_row = tok_row // half_tok ^ side
    own_sums = mix_head(jnp.stack([own_row] + chunk_at), attended, gates, out_blocks, None)
    partial_sums = mix_head(jnp.stack([1 - own_row] + chunk_at), peer, gates, out_blocks, own_sums)
    sides = [[b * half_mdl + z for z in range(half_mdl)] for b in range(2)]
    arrived = lax.all_to_all(partial_sums, "mdl", 0, 0, axis_index_groups=sides, tiled=True)
    mixed = jnp.sum(arrived.astype(jnp.float32), axis=0)
    span = width // groups
    residual = lax.dynamic_slice_in_dim(hidden, mdl_row * span, span, 1)
    output = (residual.astype(jnp.float32) + mixed).astype(jnp.bfloat16)

    cache = incoming[source].reshape(pages_here, page, 2, head_cols)
    return (output, cache)


def solution(mesh):
    placed = (
        P("tok", None),
        P(),
        P("tok", None),
        P(),
        P(),
        P(None, "tok", "mdl"),
        P(None, "tok", "mdl"),
        P(None, "mdl", "tok"),
        P("tok"),
    )
    return jax.shard_map(
        local,
        mesh=mesh,
        in_specs=placed,
        out_specs=(P("tok", "mdl"), P("tok", None, None, "mdl")),
        check_vma=False,
    )
```

```python
import functools
import math

import jax
import jax.numpy as jnp
from jax import lax
from jax.experimental import pallas as pl
from jax.experimental.pallas import tpu as pltpu
from jax.sharding import PartitionSpec as P

HDIM = 128
CHUNK = 128
LABEL_ROWS = 16
CHIPS_X = 4
WINDOW_PAIRS = 5
SEGS = 4
EPSILON = 1e-05
MASKED = -1e30
KEY_BLOCK = 512
QUERY_BLOCK = 256
QUERY_SCALE = math.log2(math.e) / math.sqrt(HDIM)


def rms_norm(hidden, norm_gain):
    values = hidden.astype(jnp.float32)
    factor = lax.rsqrt(jnp.mean(values * values, axis=-1, keepdims=True) + EPSILON)
    return (values * factor * norm_gain).astype(jnp.bfloat16)


def route_weights(normed, router_weight, routes):
    logits = jnp.dot(normed.astype(jnp.float32), router_weight, precision=lax.Precision.HIGHEST)
    expert_ids = jnp.arange(logits.shape[1], dtype=jnp.int32)
    picked = routes[:, :, None] == expert_ids[None, None, :]
    chosen = jnp.sum(jnp.where(picked, logits[:, None, :], jnp.float32(0.0)), axis=-1)
    gates = jax.nn.softmax(chosen, axis=-1)
    return jnp.where(picked, gates[:, :, None], 0.0).reshape(routes.shape[0], -1)


def cost(flops, transcendentals, moved):
    return pl.CostEstimate(flops=flops, transcendentals=transcendentals, bytes_accessed=moved)


def kv_body(core_ref, normed_ref, mine_ref, other_ref, out_ref, weight_ref):
    @pl.when(pl.program_id(0) == 0)
    def _():
        first = core_ref[0] == 0
        for k in range(mine_ref.shape[0]):
            for m in range(2):
                at = slice(m * CHUNK, (m + 1) * CHUNK)
                mine, other = mine_ref[k, at], other_ref[k, at]
                row = 2 * k * CHUNK
                weight_ref[row : row + CHUNK, at] = jnp.where(first, mine, other)
                weight_ref[row + CHUNK : row + 2 * CHUNK, at] = jnp.where(first, other, mine)

    total = jnp.dot(normed_ref[...], weight_ref[...], preferred_element_type=jnp.float32)
    out_ref[...] = total.astype(jnp.bfloat16)


def project_kv(core, normed, mine, other):
    tokens, width = normed.shape
    chips, _, cols = mine.shape
    rows = tokens // 2
    whole = pl.BlockSpec((chips, 2 * CHUNK, cols), lambda i, c: (0, 0, 0))
    return pl.pallas_call(
        kv_body,
        grid_spec=pltpu.PrefetchScalarGridSpec(
            num_scalar_prefetch=1,
            grid=(2,),
            in_specs=[pl.BlockSpec((rows, width), lambda i, c: (i, 0)), whole, whole],
            out_specs=pl.BlockSpec((rows, 2 * cols), lambda i, c: (i, 0)),
            scratch_shapes=[pltpu.VMEM((width, 2 * cols), jnp.bfloat16)],
        ),
        out_shape=jax.ShapeDtypeStruct((tokens, 2 * cols), jnp.bfloat16),
        cost_estimate=cost(2 * tokens * width * 2 * cols, 0, 2 * tokens * width),
    )(core[None], normed, mine, other)


def owners_of(tok_row, half_tok):
    core, chip, row = tok_row % 2, tok_row // 2 % CHIPS_X, tok_row // half_tok
    owners = []
    for c in range(2):
        source = core ^ c
        for step in (0, 2 * source - 1, 1 - 2 * source, 2):
            at = (chip + CHIPS_X + step) % CHIPS_X * 2 + source
            owners += [(row ^ r) * half_tok + at for r in range(2)]
    return owners


def piece_refs(refs):
    return [ref.at[row] for ref in refs for row in range(2)]


def query_body(owner_ref, normed_ref, routes_ref, *refs):
    pieces, out_ref, ordered_ref = piece_refs(refs[:-2]), refs[-2], refs[-1]
    step = pl.program_id(0)
    pair = pieces[0].shape[0]
    cols = out_ref.shape[2]

    @pl.when(step == 0)
    def _():
        for k in range(len(pieces)):
            at = pl.ds(pl.multiple_of(owner_ref[k] * CHUNK, CHUNK), CHUNK)
            ordered_ref[:, k * CHUNK : (k + 1) * CHUNK] = normed_ref[:, at]

    weights = [jnp.concatenate([ref[k] for ref in pieces], axis=0) for k in range(pair)]
    total = jnp.dot(
        ordered_ref[...], jnp.concatenate(weights, axis=1), preferred_element_type=jnp.float32
    )
    for s in range(out_ref.shape[0]):
        route = routes_ref[:, s : s + 1]
        value = out_ref[s]
        for k in range(pair):
            mine = (total[:, k * cols : (k + 1) * cols] * QUERY_SCALE).astype(jnp.bfloat16)
            value = jnp.where(route == step * pair + k, mine, value)
        out_ref[s] = value


def project_queries(owners, normed, blocks, routes):
    tokens, width = normed.shape
    experts, rows, cols = blocks[0].shape[1:]
    return pl.pallas_call(
        query_body,
        grid_spec=pltpu.PrefetchScalarGridSpec(
            num_scalar_prefetch=1,
            grid=(experts // 2,),
            in_specs=[
                pl.BlockSpec((tokens, width), lambda e, r: (0, 0)),
                pl.BlockSpec(routes.shape, lambda e, r: (0, 0)),
            ]
            + [
                pl.BlockSpec((2, 2, rows, cols), lambda e, r: (0, e, 0, 0))
                for _ in blocks
            ],
            out_specs=pl.BlockSpec((routes.shape[1], tokens, cols), lambda e, r: (0, 0, 0)),
            scratch_shapes=[pltpu.VMEM((tokens, width), jnp.bfloat16)],
        ),
        out_shape=jax.ShapeDtypeStruct((routes.shape[1], tokens, cols), jnp.bfloat16),
        cost_estimate=cost(2 * tokens * width * experts * cols, 0, 4 * normed.size),
    )(owners, normed, routes, *blocks)


def attend_body(bounds_ref, q_ref, lower_ref, place_ref, *refs):
    block_refs, out_ref, kv_ref = refs[:-2], refs[-2], refs[-1]
    step = pl.program_id(0)
    routes, tokens, dim = q_ref.shape
    rows = routes * tokens
    half = len(block_refs) // 2
    core = bounds_ref[bounds_ref.shape[0] - 1]

    @pl.when(step == 0)
    def _():
        for k, ref in enumerate(block_refs):
            kv_ref[k] = ref[...]

    q = q_ref[...].reshape(rows, dim)
    lower = jnp.concatenate([lower_ref[...]] * routes, axis=0)
    place = jnp.concatenate([place_ref[...]] * routes, axis=0)

    def block(masked, at, carry):
        peak, total, accum = carry
        first = at * KEY_BLOCK
        slot = jnp.where(at % 2 == core, 0, half) + at // 2
        keys = kv_ref[slot, :, :dim]
        values = kv_ref[slot, :, dim:]
        scores = lax.dot_general(
            q, keys, (((1,), (1,)), ((), ())), preferred_element_type=jnp.float32
        )
        if masked:
            key_place = first + lax.broadcasted_iota(jnp.int32, (1, KEY_BLOCK), 1)
            allowed = (key_place >= lower) & (key_place <= place)
            scores = jnp.where(allowed, scores, MASKED)
        new_peak = jnp.maximum(peak, jnp.max(scores, axis=1, keepdims=True))
        shrink = jnp.exp2(peak - new_peak)
        expon = jnp.exp2(scores - new_peak)
        total = total * shrink + jnp.sum(expon, axis=1, keepdims=True)
        accum = accum * shrink + jnp.dot(
            expon.astype(jnp.bfloat16), values, preferred_element_type=jnp.float32
        )
        return new_peak, total, accum

    state = (
        jnp.full((rows, 1), MASKED, jnp.float32),
        jnp.zeros((rows, 1), jnp.float32),
        jnp.zeros((rows, dim), jnp.float32),
    )
    start, full, edge, stop = (bounds_ref[4 * step + k] for k in range(4))
    state = lax.fori_loop(start, full, lambda at, c: block(True, at, c), state)
    state = lax.fori_loop(full, edge, lambda at, c: block(False, at, c), state)
    state = lax.fori_loop(edge, stop, lambda at, c: block(True, at, c), state)
    out_ref[...] = (state[2] / state[1]).astype(jnp.bfloat16).reshape(routes, tokens, dim)


def attend(queries, lower, place, core, blocks):
    routes, tokens, dim = queries.shape
    steps = tokens // QUERY_BLOCK
    first_lower = lower.reshape(steps, QUERY_BLOCK)[:, 0]
    last_lower = lower.reshape(steps, QUERY_BLOCK)[:, -1]
    first_place = place.reshape(steps, QUERY_BLOCK)[:, 0]
    last_place = place.reshape(steps, QUERY_BLOCK)[:, -1]
    start = first_lower // KEY_BLOCK
    stop = last_place // KEY_BLOCK + 1
    full = jnp.clip((last_lower + KEY_BLOCK - 1) // KEY_BLOCK, start, stop)
    edge = jnp.clip((first_place + 1) // KEY_BLOCK, full, stop)
    bounds = jnp.concatenate([jnp.stack([start, full, edge, stop], axis=1).reshape(-1), core[None]])
    return pl.pallas_call(
        attend_body,
        grid_spec=pltpu.PrefetchScalarGridSpec(
            num_scalar_prefetch=1,
            grid=(steps,),
            in_specs=[
                pl.BlockSpec((routes, QUERY_BLOCK, dim), lambda i, b: (0, i, 0)),
                pl.BlockSpec((QUERY_BLOCK, 1), lambda i, b: (i, 0)),
                pl.BlockSpec((QUERY_BLOCK, 1), lambda i, b: (i, 0)),
            ]
            + [pl.BlockSpec(block.shape, lambda i, b: (0, 0)) for block in blocks],
            out_specs=pl.BlockSpec((routes, QUERY_BLOCK, dim), lambda i, b: (0, i, 0)),
            scratch_shapes=[pltpu.VMEM((len(blocks),) + blocks[0].shape, jnp.bfloat16)],
        ),
        out_shape=jax.ShapeDtypeStruct((routes, tokens, dim), jnp.bfloat16),
        cost_estimate=cost(
            2 * routes * tokens * tokens * len(blocks) * dim,
            routes * tokens * tokens * len(blocks) // 2,
            4 * len(blocks) * tokens * dim,
        ),
    )(bounds, queries, lower[:, None], place[:, None], *blocks)


def mix_body(has_start, at_ref, head_ref, gates_ref, *refs):
    blocks, out_ref, mix_ref = refs[:8], refs[-2], refs[-1]
    start_ref = refs[8] if has_start else None
    _, experts, rows, cols = blocks[0].shape
    routes = head_ref.shape[0]
    attended = [head_ref[s].astype(jnp.float32) for s in range(routes)]
    for e in range(experts):
        value = sum(
            attended[s] * gates_ref[:, s * experts + e : s * experts + e + 1]
            for s in range(routes)
        )
        mix_ref[:, e * rows : (e + 1) * rows] = value.astype(jnp.bfloat16)
    for step in range(CHIPS_X):
        weight = jnp.concatenate(
            [blocks[c * CHIPS_X + step][0].reshape(experts * rows, cols) for c in range(2)], axis=1
        )
        total = jnp.dot(mix_ref[...], weight, preferred_element_type=jnp.float32)
        for c in range(2):
            k = c * CHIPS_X + step
            part = total[:, c * cols : (c + 1) * cols]
            if has_start:
                part = part + start_ref[k]
                out_ref[at_ref[1 + k]] = part.astype(out_ref.dtype)
            else:
                out_ref[k] = part


def mix_head(at, head, gates, blocks, start):
    routes, tokens, dim = head.shape
    experts, rows, cols = blocks[0].shape[1:]
    whole = lambda i, s: (0, 0, 0)
    shape = (2 * CHIPS_X, tokens, cols)
    extra = [] if start is None else [start]
    return pl.pallas_call(
        functools.partial(mix_body, start is not None),
        grid_spec=pltpu.PrefetchScalarGridSpec(
            num_scalar_prefetch=1,
            grid=(1,),
            in_specs=[
                pl.BlockSpec((routes, tokens, dim), whole),
                pl.BlockSpec(gates.shape, lambda i, s: (0, 0)),
            ]
            + [
                pl.BlockSpec((1, experts, rows, cols), lambda i, s: (s[0], 0, 0, 0))
                for _ in blocks
            ]
            + [pl.BlockSpec(shape, whole) for _ in extra],
            out_specs=pl.BlockSpec(shape, whole),
            scratch_shapes=[pltpu.VMEM((tokens, experts * rows), jnp.bfloat16)],
        ),
        out_shape=jax.ShapeDtypeStruct(shape, jnp.float32 if start is None else jnp.bfloat16),
        cost_estimate=cost(
            2 * tokens * experts * rows * 2 * CHIPS_X * cols, 0, 16 * blocks[0].size
        ),
    )(at, head, gates, *blocks, *extra)


def local(
    hidden,
    segment_ids,
    routes,
    norm_gain,
    router_weight,
    query_weight,
    kv_weight,
    out_weight,
    page_table,
):
    tok_dev, width = hidden.shape
    experts, chunk, head_cols = query_weight.shape
    shards = lax.axis_size("tok")
    groups = lax.axis_size("mdl")
    half_tok, half_mdl = shards // 2, groups // 2
    tok_row = lax.axis_index("tok")
    mdl_row = lax.axis_index("mdl")
    core = tok_row % 2
    side = mdl_row // half_mdl

    core_swap = [(i, i ^ 1) for i in range(shards)]

    def along_x(block, sign):
        moves = []
        for i in range(shards):
            chip = (i // 2 % CHIPS_X + sign * (1 - i % 2 * 2)) % CHIPS_X
            moves.append((i, i // half_tok * half_tok + chip * 2 + i % 2))
        return lax.ppermute(block, "tok", moves)

    def both_cores(blocks):
        return blocks + [lax.ppermute(block, "tok", core_swap) for block in blocks]

    other_row = lax.ppermute(
        query_weight, "tok", [(i, (i + half_tok) % shards) for i in range(shards)]
    )

    pages_here = page_table.shape[0]
    labels = jnp.stack([page_table // pages_here, page_table % pages_here]).astype(jnp.bfloat16)
    piece = jnp.concatenate(
        [
            kv_weight.reshape(-1, head_cols),
            jnp.pad(labels, ((0, LABEL_ROWS - 2), (0, head_cols - pages_here))),
        ],
        axis=0,
    )
    same_core = [[2 * k + c for k in range(half_tok)] for c in range(2)]
    kv_mine = lax.all_to_all(
        jnp.broadcast_to(piece[None], (half_tok,) + piece.shape),
        "tok", 0, 0, axis_index_groups=same_core, tiled=True,
    )
    kv_other = lax.ppermute(kv_mine, "tok", core_swap)
    normed = rms_norm(hidden, norm_gain)
    query_own, _ = lax.optimization_barrier((jnp.stack([query_weight, other_row]), kv_mine))
    query_near, query_next = along_x(query_own, 1), along_x(query_own, -1)
    key_values = project_kv(core, normed, kv_mine, kv_other)

    near, _ = lax.optimization_barrier((query_near, key_values))
    query_far = along_x(near, 1)

    earlier = [
        lax.ppermute(key_values, "tok", [(i, i + 2 * s) for i in range(shards - 2 * s)])
        for s in range(WINDOW_PAIRS - 1, 0, -1)
    ]
    page = tok_dev // pages_here
    per_peer = pages_here // shards
    page_ids = jnp.arange(pages_here, dtype=jnp.int32)
    before = page_ids[:, None] > page_ids[None, :]
    targets = page_table // pages_here
    rank = jnp.sum(((targets[:, None] == targets[None, :]) & before).astype(jnp.int32), axis=1)
    slot = targets * per_peer + rank
    listing = jnp.sum(jnp.where(slot[None, :] == page_ids[:, None], page_ids[None, :], 0), axis=1)
    outgoing = key_values.reshape(pages_here, page, 2 * head_cols)[listing]
    incoming = lax.all_to_all(outgoing, "tok", 0, 0, tiled=True)
    got = jnp.concatenate([kv_mine, kv_other])[:, 2 * CHUNK : 2 * CHUNK + 2, :pages_here]
    chips = jnp.arange(half_tok, dtype=jnp.int32) * 2
    senders = jnp.concatenate([chips + core, chips + 1 - core])
    target = got[:, 0] == tok_row.astype(jnp.bfloat16)
    order = jnp.sum((target[:, None, :] & before[None]).astype(jnp.int32), axis=2)
    chosen = target[None] & (got[None, :, 1] == page_ids.astype(jnp.bfloat16)[:, None, None])
    source = jnp.sum(jnp.where(chosen, (senders[:, None] * per_peer + order)[None], 0), axis=(1, 2))

    out_early, _ = lax.optimization_barrier((out_weight, kv_mine))

    def along_y(step):
        moves = []
        for a in range(2):
            for b in range(2):
                for i in range(half_tok):
                    for z in range(half_mdl):
                        source = (a * half_tok + i) * groups + (b ^ step) * half_mdl + z
                        moves.append((source, (b * half_tok + i) * groups + a * half_mdl + z))
        return lax.ppermute(out_early, ("tok", "mdl"), moves)

    out_own = jnp.stack([along_y(0), along_y(1)])
    earlier, out_own, incoming, late_normed = lax.optimization_barrier(
        (earlier, out_own, incoming, normed)
    )
    mine = earlier + [key_values]
    window = mine + [lax.ppermute(block, "tok", core_swap) for block in mine]

    query_blocks = both_cores([query_own, query_near, query_next, query_far])
    out_near, out_next = along_x(out_own, 1), along_x(out_own, -1)

    window_first = (tok_row // 2 - (WINDOW_PAIRS - 1)) * 2 * tok_dev
    own_first = tok_row * tok_dev
    own_segments = lax.dynamic_slice_in_dim(segment_ids, own_first, tok_dev)
    prompt_ids = jnp.arange(SEGS, dtype=jnp.int32)
    seg_first = jnp.sum((segment_ids[:, None] < prompt_ids[None, :]).astype(jnp.int32), axis=0)
    lower = jnp.sum(
        jnp.where(own_segments[:, None] == prompt_ids[None, :], seg_first[None, :], 0), axis=1
    )
    place = own_first + jnp.arange(tok_dev, dtype=jnp.int32)
    gates = route_weights(late_normed, router_weight, routes)

    owners = owners_of(tok_row, half_tok)
    queries = project_queries(jnp.stack(owners), normed, query_blocks, routes)
    queries, out_near, out_next = lax.optimization_barrier((queries, out_near, out_next))
    out_blocks = both_cores([out_own, out_near, out_next, along_x(out_near, 1)])
    attended = attend(queries, lower - window_first, place - window_first, core, window)
    peer = lax.ppermute(attended, "mdl", [(j, j ^ half_mdl) for j in range(groups)])
    chunk_at = [owner % half_tok for owner in owners[::2]]
    own_row = tok_row // half_tok ^ side
    own_sums = mix_head(jnp.stack([own_row] + chunk_at), attended, gates, out_blocks, None)
    partial_sums = mix_head(jnp.stack([1 - own_row] + chunk_at), peer, gates, out_blocks, own_sums)
    sides = [[b * half_mdl + z for z in range(half_mdl)] for b in range(2)]
    arrived = lax.all_to_all(partial_sums, "mdl", 0, 0, axis_index_groups=sides, tiled=True)
    mixed = jnp.sum(arrived.astype(jnp.float32), axis=0)
    span = width // groups
    residual = lax.dynamic_slice_in_dim(hidden, mdl_row * span, span, 1)
    output = (residual.astype(jnp.float32) + mixed).astype(jnp.bfloat16)

    cache = incoming[source].reshape(pages_here, page, 2, head_cols)
    return (output, cache)


def solution(mesh):
    placed = (
        P("tok", None),
        P(),
        P("tok", None),
        P(),
        P(),
        P(None, "tok", "mdl"),
        P(None, "tok", "mdl"),
        P(None, "mdl", "tok"),
        P("tok"),
    )
    return jax.shard_map(
        local,
        mesh=mesh,
        in_specs=placed,
        out_specs=(P("tok", "mdl"), P("tok", None, None, "mdl")),
        check_vma=False,
    )
```
